128 devices in a mesh: tm: 16 (over x_hi, z, core), space: 8 (over x_lo, y).
Axes of the slice: x: 4 (x_hi: 2, x_lo: 2; x = x_hi * 2 + x_lo), y: 4, z: 4, core: 2. Of those that a mesh axis runs over, the one named last changes fastest.
Arguments:
- velocity: float32 [256, 3, 48, 2304], P('tm', None, 'space'), may hold values from -2.4 to 2.4
- period: float32 [1], replicated, may hold values from 40 to 80
- wavenumber: int32 [1], replicated, may hold values from 1 to 23
Outputs:
- new_field: float32 [256, 3, 48, 2304], P('tm', None, 'space')
- residual: float32 [256, 3, 48, 2304], P('tm', None, 'space')
- period_grad: float32 [1], replicated
The draws below stay inside these ranges and needn't reach their ends.
All inputs are finite; a program needn't handle non-finite values.
Results may differ from the reference program's by a relative error of at most 0.0003.
Values sent between devices are 32-bit elements; how exact they have to be, the bound alone decides.
No kernel may reach another device: no remote copies, remote signals or barrier semaphores. Data moves between devices by JAX's collectives and lax.ppermute only.
A program may use at most 128 MiB of HBM per device.

```python
import math
import jax
import jax.numpy as jnp
from jax import lax

NY = 48
NZ = 48
NT = 256
NX = 48


def draw_velocity(key, part):
    field_shape = (NT, 3, NX, NY * NZ)
    subkeys = jax.random.split(key, 4)
    level_index = jnp.arange(NT, dtype=jnp.int32)
    phase_index = level_index % 3
    cell_index = jnp.arange(NX, dtype=jnp.int32)
    cell_share = cell_index.astype(jnp.float32) / max(NX - 1, 1)
    moved_cells = (cell_index[None, :] - level_index[:, None]) % NX
    component_index = jnp.arange(3, dtype=jnp.int32)
    low_level = 0.25
    middle_level = 0.6
    high_level = 0.95
    pattern = jnp.clip(0.4 * jax.random.normal(subkeys[1], field_shape[1:], jnp.float32), -0.75, 0.75)
    wave_row = jnp.clip(0.4 * jax.random.normal(subkeys[2], (NX,), jnp.float32), -0.75, 0.75)
    noise_field = jnp.clip(0.15 * jax.random.normal(subkeys[3], field_shape, jnp.float32), -0.3, 0.3)
    envelope = 0.5 + 0.5 * cell_share
    drift_speed = 0.5
    jitter = jax.random.uniform(subkeys[0], (NT,), jnp.float32, -0.05, 0.05)
    amplitude = jnp.where(phase_index == 0, low_level, jnp.where(phase_index == 1, middle_level, high_level)) + jitter
    travel = wave_row[moved_cells]
    fluctuation = amplitude[:, None, None, None] * pattern[None] + noise_field
    along_second = (component_index == 1).astype(jnp.float32)
    fluctuation = fluctuation + along_second[None, :, None, None] * travel[:, None, :, None]
    along_first = (component_index == 0).astype(jnp.float32)
    drift = drift_speed * along_first[None, :, None, None]
    return drift + envelope[None, None, :, None] * fluctuation


def setup_inputs(seed: int = 0) -> dict:
    key_of = jax.random.split(jax.random.key(seed), 4)
    velocity = draw_velocity(jax.random.fold_in(key_of[3], 71), 0)
    period = jnp.clip(jax.random.uniform(key_of[1], (1,), jnp.float32, 40.0, 80.0), 40.0, 80.0)
    wavenumber = jax.random.randint(key_of[2], (1,), 1, NY // 2).astype(jnp.int32)
    return {"velocity": velocity, "period": period, "wavenumber": wavenumber}


weights = (0.8, -0.2, 4.0 / 105.0, -1.0 / 280.0)
viscosity = 0.02
step_size = 0.15


def rate_in_time(values, inverse_step):
    out_levels = values.shape[0] - 8
    summed = jnp.zeros((out_levels,) + values.shape[1:], jnp.float32)
    for offset, weight in enumerate(weights, 1):
        summed = summed + weight * (values[4 + offset:4 + offset + out_levels] - values[4 - offset:4 - offset + out_levels])
    return summed * inverse_step


def along_first(values, spacing):
    return (values[:, :, 2:] - values[:, :, :-2]) / (2.0 * spacing)


def along_axis(values, axis_number, spacing):
    return (jnp.roll(values, -1, axis_number) - jnp.roll(values, 1, axis_number)) / (2.0 * spacing)


def laplace(padded, spacings):
    center = padded[:, :, 1:-1]
    result = (padded[:, :, 2:] + padded[:, :, :-2] - 2.0 * center) / spacings[0] ** 2
    for axis_number, spacing in ((3, spacings[1]), (4, spacings[2])):
        result = result + (jnp.roll(center, -1, axis_number) + jnp.roll(center, 1, axis_number) - 2.0 * center) / spacing ** 2
    return result


def forcing_term(wavenumber):
    row_index = jnp.arange(NY, dtype=jnp.float32)
    profile = jnp.sin(wavenumber[0].astype(jnp.float32) * (2.0 * math.pi / NY) * row_index)
    return jnp.stack([profile, 0.0 * profile, 0.0 * profile]).reshape(1, 3, 1, NY, 1)


def residual_parts(flow_levels, flow_slabs, inverse_step, spacings, forcing):
    level_rate = rate_in_time(flow_levels, inverse_step)
    center = flow_slabs[:, :, 1:-1]
    gradients = (along_first(flow_slabs, spacings[0]), along_axis(center, 3, spacings[1]), along_axis(center, 4, spacings[2]))
    advect = center[:, 0:1] * gradients[0] + center[:, 1:2] * gradients[1] + center[:, 2:3] * gradients[2]
    residue = level_rate + advect - viscosity * laplace(flow_slabs, spacings) - forcing
    return residue, level_rate, gradients


def descent_direction(residue_levels, residue_slabs, flow_near, gradients, inverse_step, spacings):
    residue_center = residue_slabs[:, :, 1:-1]
    flow_center = flow_near[:, :, 1:-1]
    result = -rate_in_time(residue_levels, inverse_step)
    result = result - along_first(flow_near[:, 0:1] * residue_slabs, spacings[0])
    result = result - along_axis(flow_center[:, 1:2] * residue_center, 3, spacings[1])
    result = result - along_axis(flow_center[:, 2:3] * residue_center, 4, spacings[2])
    result = result + jnp.stack([jnp.sum(residue_center * gradient, axis=1) for gradient in gradients], axis=1)
    result = result - viscosity * laplace(residue_slabs, spacings)
    return result


def reference(velocity, period, wavenumber):
    inverse_step = NT / period[0]
    spacings = (2.0 * math.pi / NX, 2.0 * math.pi / NY, 2.0 * math.pi / NZ)
    forcing = forcing_term(wavenumber)
    shaped = velocity.reshape(NT, 3, NX, NY, NZ)
    wrapped = jnp.concatenate([shaped[NT - 8:], shaped, shaped[:8]], 0)
    wrapped = jnp.concatenate([wrapped[:, :, NX - 2:], wrapped, wrapped[:, :, :2]], 2)

    def one_block(block_number):
        first_level = (block_number * 8).astype(jnp.int32)
        window = lax.dynamic_slice_in_dim(wrapped, first_level, 24, 0)
        residue, level_rate, gradients = residual_parts(window[:, :, 1:-1], window[4:-4], inverse_step, spacings, forcing)
        residue_center = residue[4:-4, :, 1:-1]
        rate_center = level_rate[4:-4, :, 1:-1]
        near_gradients = tuple(gradient[4:-4, :, 1:-1] for gradient in gradients)
        descent = descent_direction(residue[:, :, 1:-1], residue[4:-4], window[8:-8, :, 1:-1], near_gradients, inverse_step, spacings)
        sums = jnp.stack([jnp.sum(residue_center * rate_center), jnp.sum(rate_center * rate_center), jnp.sum(descent * rate_center)])
        return residue_center, rate_center, descent, sums

    blocks = lax.map(one_block, jnp.arange(NT // 8, dtype=jnp.int32))
    residual = blocks[0].reshape(NT, 3, NX, NY * NZ)
    level_rate = blocks[1].reshape(NT, 3, NX, NY * NZ)
    descent = blocks[2].reshape(NT, 3, NX, NY * NZ)
    sums = jnp.sum(blocks[3], axis=0)
    shift_weight = sums[2] / sums[1]
    new_field = velocity - step_size * (descent - shift_weight * level_rate)
    cell_count = 3.0 * NT * NX * NY * NZ
    period_grad = (-sums[0] / (period[0] * cell_count)).reshape(1)
    return new_field, residual, period_grad
```

```python
import math

import jax
import jax.numpy as jnp
from jax import lax
from jax.experimental import pallas as pl
from jax.experimental.pallas import tpu as pltpu
from jax.sharding import Mesh
from jax.sharding import PartitionSpec as P

NY = 48
NZ = 48
NC = NY * NZ
LANES = 128
NJ = NC // LANES
TM = ("tm_0", "tm_1", "tm_2")
SPACE = ("space_0", "space_1")
ALL = TM + SPACE

weights = (0.8, -0.2, 4.0 / 105.0, -1.0 / 280.0)
viscosity = 0.02
step_size = 0.15

ROWS = 32
OWN = 8


def cols(j):
    return pl.ds(j * LANES, LANES)


def roll(x, shift):
    return pltpu.roll(x, shift % LANES, x.ndim - 1)


class Shifts:
    def __init__(self, shape):
        self.lane = lax.broadcasted_iota(jnp.int32, shape, len(shape) - 1)

    def y_next(self, here, after):
        return roll(jnp.where(self.lane < NZ, after, here), -NZ)

    def y_prev(self, before, here):
        return roll(jnp.where(self.lane >= LANES - NZ, before, here), NZ)

    def column(self, j, value):
        base = (j * LANES) % NZ
        mask = None
        for lane in range(LANES):
            if (base + lane) % NZ == value:
                one = self.lane == lane
                mask = one if mask is None else jnp.logical_or(mask, one)
        return mask

    def z_next(self, j, before, here, after):
        base = (j * LANES) % NZ
        straight = here if (base + LANES) % NZ == 0 else jnp.where(self.lane == 0, after, here)
        first = (NZ - 1 - base) % NZ
        wrap = here if first >= NZ - 1 else jnp.where(self.lane >= LANES - (NZ - 1), before, here)
        return jnp.where(self.column(j, NZ - 1), roll(wrap, NZ - 1), roll(straight, -1))

    def z_prev(self, j, before, here, after):
        base = (j * LANES) % NZ
        straight = here if base == 0 else jnp.where(self.lane == LANES - 1, before, here)
        last = LANES - 1 - (base + LANES - 1) % NZ
        wrap = here if last + NZ - 1 < LANES else jnp.where(self.lane < NZ - 1, after, here)
        return jnp.where(self.column(j, 0), roll(wrap, -(NZ - 1)), roll(straight, 1))


def rate(ref, c, x, j, levels, scaled):
    total = None
    for m in range(1, 5):
        ahead = ref[c, x, j, pl.ds(OWN + m, levels), :]
        behind = ref[c, x, j, pl.ds(OWN - m, levels), :]
        term = scaled[m - 1] * (ahead - behind)
        total = term if total is None else total + term
    return total


def fill(scratch, own, low, high, left, right):
    slabs, levels = own.shape[1], own.shape[2]

    def slab(x, carry):
        for c in range(3):
            for j in range(NJ):
                scratch[c, x + 1, j, pl.ds(OWN, levels), :] = own[c, x, :, cols(j)]
                scratch[c, x + 1, j, pl.ds(OWN - 4, 4), :] = low[c, x, :, cols(j)]
                scratch[c, x + 1, j, pl.ds(OWN + levels, 4), :] = high[c, x, :, cols(j)]
        return carry

    lax.fori_loop(0, slabs, slab, 0)
    for c in range(3):
        for j in range(NJ):
            scratch[c, 0, j, pl.ds(OWN, levels), :] = left[c, :, cols(j)]
            scratch[c, slabs + 1, j, pl.ds(OWN, levels), :] = right[c, :, cols(j)]


def residual_kernel(spacing, scale, own, low, high, left, right, forcing, res, rt, grad, scratch):
    levels = own.shape[2]
    x = pl.program_id(0)

    @pl.when(x == 0)
    def _():
        fill(scratch, own, low, high, left, right)

    scaled = [w * scale[0] for w in weights]
    alpha = 1.0 / (2.0 * spacing)
    beta = viscosity / spacing**2
    sh = Shifts((levels, LANES))

    def at(c, dx, j):
        return scratch[c, x + 1 + dx, j % NJ, pl.ds(OWN, levels), :]

    for j in range(NJ):
        vel = [alpha * at(a, 0, j) for a in range(3)]
        for c in range(3):
            here, before, after = at(c, 0, j), at(c, 0, j - 1), at(c, 0, j + 1)
            pairs = (
                (at(c, 1, j), at(c, -1, j)),
                (sh.y_next(here, after), sh.y_prev(before, here)),
                (sh.z_next(j, before, here, after), sh.z_prev(j, before, here, after)),
            )
            q = rate(scratch, c, x + 1, j, levels, scaled)
            total = q + (6.0 * beta) * here
            near = None
            for a, (nxt, prv) in enumerate(pairs):
                diff = nxt - prv
                grad[a * 3 + c, 0, :, cols(j)] = diff
                total = total + vel[a] * diff
                both = nxt + prv
                near = both if near is None else near + both
            total = total - beta * near
            if c == 0:
                total = total - forcing[:, cols(j)]
            res[c, 0, :, cols(j)] = total
            rt[c, 0, :, cols(j)] = q


def descent_kernel(spacing, scale, own, rt, grad, left0, right0, res, low, high, left, right, base, sums, scratch, flow, acc):
    levels = own.shape[2]
    slabs = own.shape[1]
    x = pl.program_id(0)
    alpha = 1.0 / (2.0 * spacing)
    beta = viscosity / spacing**2

    @pl.when(x == 0)
    def _():
        fill(scratch, res, low, high, left, right)
        flow[0] = alpha * left0[...]
        flow[slabs + 1] = alpha * right0[...]

        def slab(i, carry):
            flow[i + 1] = alpha * own[0, i]
            return carry

        lax.fori_loop(0, slabs, slab, 0)
        acc[...] = jnp.zeros_like(acc)

    scaled = [w * scale[0] for w in weights]
    sh = Shifts((levels, LANES))

    def at(c, dx, j):
        return scratch[c, x + 1 + dx, j % NJ, pl.ds(OWN, levels), :]

    s1 = s2 = s3 = None
    for c in range(3):
        cache = {}

        def products(j):
            j = j % NJ
            if j not in cache:
                value = at(c, 0, j)
                y = (alpha * own[1, x, :, cols(j)]) * value
                z = (alpha * own[2, x, :, cols(j)]) * value
                s = beta * value
                cache[j] = (y + s, y - s, z + s, z - s)
            return cache[j]

        for j in range(NJ):
            here = at(c, 0, j)
            (yp0, ym0, zp0, zm0) = products(j - 1)
            (yp1, ym1, zp1, zm1) = products(j)
            (yp2, ym2, zp2, zm2) = products(j + 1)
            total = (6.0 * beta) * here - rate(scratch, c, x + 1, j, levels, scaled)
            nxt, prv = at(c, 1, j), at(c, -1, j)
            total = total - (flow[x + 2, :, cols(j)] + beta) * nxt
            total = total + (flow[x, :, cols(j)] - beta) * prv
            total = total - sh.y_next(yp1, yp2) + sh.y_prev(ym0, ym1)
            total = total - sh.z_next(j, zp0, zp1, zp2) + sh.z_prev(j, zm0, zm1, zm2)
            dots = None
            for k in range(3):
                term = at(k, 0, j) * grad[c * 3 + k, 0, :, cols(j)]
                dots = term if dots is None else dots + term
            total = total + alpha * dots
            q = rt[c, 0, :, cols(j)]
            t1, t2, t3 = here * q, q * q, total * q
            s1 = t1 if s1 is None else s1 + t1
            s2 = t2 if s2 is None else s2 + t2
            s3 = t3 if s3 is None else s3 + t3
            base[c, 0, :, cols(j)] = own[c, x, :, cols(j)] - step_size * total
    acc[0] += s1
    acc[1] += s2
    acc[2] += s3

    @pl.when(x == slabs - 1)
    def _():
        lane = lax.broadcasted_iota(jnp.int32, (1, LANES), 1)
        row = jnp.zeros((1, LANES), jnp.float32)
        for k in range(3):
            row = jnp.where(lane == k, jnp.sum(acc[k]), row)
        sums[...] = jnp.broadcast_to(row[None], sums.shape)


def update_kernel(cells, period, gathered, base, rt, out, pgrad):
    row = jnp.sum(gathered[...], axis=0)
    s1, s2, s3 = row[0, 0], row[0, 1], row[0, 2]
    weight = jnp.full((1, LANES), step_size * s3, jnp.float32) / jnp.full((1, LANES), s2, jnp.float32)
    weight = weight[0, 0]
    out[...] = base[...] + weight * rt[...]

    @pl.when(pl.program_id(0) == 0)
    def _():
        pgrad[...] = jnp.full((1, LANES), -s1, jnp.float32) / jnp.full((1, LANES), period[0] * cells, jnp.float32)


def halo(array, axis, dim, width):
    count, length = lax.axis_size(axis), array.shape[dim]
    up = [(i, (i + 1) % count) for i in range(count)]
    down = [(j, i) for i, j in up]
    last = lax.slice_in_dim(array, length - width, length, axis=dim)
    first = lax.slice_in_dim(array, 0, width, axis=dim)
    return lax.ppermute(last, axis, up), lax.ppermute(first, axis, down)


def halos(array):
    low, high = halo(array, TM, 2, 4)
    left, right = halo(array, SPACE, 1, 1)
    return low, high, left[:, 0], right[:, 0]


def on_device(velocity, period, wavenumber):
    levels, _, slabs, _ = velocity.shape
    devices = lax.axis_size(ALL)
    total_levels = levels * lax.axis_size(TM)
    grid_first = slabs * lax.axis_size(SPACE)
    spacing = 2.0 * math.pi / NY
    u = jnp.transpose(velocity, (1, 2, 0, 3))
    scale = total_levels / period
    row_index = jnp.arange(NY, dtype=jnp.float32)
    profile = jnp.sin(wavenumber[0].astype(jnp.float32) * (2.0 * math.pi / NY) * row_index)
    forcing = jnp.repeat(profile, NZ).reshape(1, NC)

    vmem = pl.BlockSpec(memory_space=pltpu.VMEM)
    smem = pl.BlockSpec(memory_space=pltpu.SMEM)
    slab3 = pl.BlockSpec((3, 1, levels, NC), lambda i: (0, i, 0, 0))
    slab9 = pl.BlockSpec((9, 1, levels, NC), lambda i: (0, i, 0, 0))
    field = jax.ShapeDtypeStruct((3, slabs, levels, NC), jnp.float32)
    padded = pltpu.VMEM((3, slabs + 2, NJ, ROWS, LANES), jnp.float32)

    low, high, left, right = halos(u)
    res, rt, grad = pl.pallas_call(
        lambda *refs: residual_kernel(spacing, *refs),
        grid=(slabs,),
        in_specs=[smem] + [vmem] * 6,
        out_specs=[slab3, slab3, slab9],
        out_shape=[field, field, jax.ShapeDtypeStruct((9, slabs, levels, NC), jnp.float32)],
        scratch_shapes=[padded],
        name="residual",
    )(scale, u, low, high, left, right, forcing)

    rlow, rhigh, rleft, rright = halos(res)
    base, sums = pl.pallas_call(
        lambda *refs: descent_kernel(spacing, *refs),
        grid=(slabs,),
        in_specs=[smem, vmem, slab3, slab9] + [vmem] * 7,
        out_specs=[slab3, pl.BlockSpec((devices, 1, LANES), lambda i: (0, 0, 0))],
        out_shape=[field, jax.ShapeDtypeStruct((devices, 1, LANES), jnp.float32)],
        scratch_shapes=[
            padded,
            pltpu.VMEM((slabs + 2, levels, NC), jnp.float32),
            pltpu.VMEM((3, levels, LANES), jnp.float32),
        ],
        name="descent",
    )(scale, u, rt, grad, left[0], right[0], res, rlow, rhigh, rleft, rright)

    gathered = lax.all_to_all(sums, ALL, 0, 0)
    cells = 3.0 * total_levels * grid_first * NY * NZ
    updated, pgrad = pl.pallas_call(
        lambda *refs: update_kernel(cells, *refs),
        grid=(slabs,),
        in_specs=[smem, vmem, slab3, slab3],
        out_specs=[slab3, pl.BlockSpec((1, LANES), lambda i: (0, 0))],
        out_shape=[field, jax.ShapeDtypeStruct((1, LANES), jnp.float32)],
        name="update",
    )(period, gathered, base, rt)
    back = (2, 0, 1, 3)
    return jnp.transpose(updated, back), jnp.transpose(res, back), pgrad[0, :1]


def solution(mesh):
    split = Mesh(mesh.devices.reshape(2, 4, 2, 2, 4), ALL)
    in_specs = (P(TM, None, SPACE, None), P(), P())
    out_specs = (P(TM, None, SPACE, None), P(TM, None, SPACE, None), P())
    return jax.shard_map(on_device, mesh=split, in_specs=in_specs, out_specs=out_specs, check_vma=False)
```

```python
import math

import jax
import jax.numpy as jnp
from jax import lax
from jax.experimental import pallas as pl
from jax.experimental.pallas import tpu as pltpu
from jax.sharding import Mesh
from jax.sharding import PartitionSpec as P

NY = 48
NZ = 48
NC = NY * NZ
LANES = 128
NJ = NC // LANES
TM = ("tm_0", "tm_1", "tm_2")
SPACE = ("space_0", "space_1")
ALL = TM + SPACE

weights = (0.8, -0.2, 4.0 / 105.0, -1.0 / 280.0)
viscosity = 0.02
step_size = 0.15

ROWS = 32
OWN = 8


def cols(j):
    return pl.ds(j * LANES, LANES)


def roll(x, shift):
    return pltpu.roll(x, shift % LANES, x.ndim - 1)


class Shifts:
    def __init__(self, shape):
        self.lane = lax.broadcasted_iota(jnp.int32, shape, len(shape) - 1)

    def y_next(self, here, after):
        return roll(jnp.where(self.lane < NZ, after, here), -NZ)

    def y_prev(self, before, here):
        return roll(jnp.where(self.lane >= LANES - NZ, before, here), NZ)

    def column(self, j, value):
        base = (j * LANES) % NZ
        mask = None
        for lane in range(LANES):
            if (base + lane) % NZ == value:
                one = self.lane == lane
                mask = one if mask is None else jnp.logical_or(mask, one)
        return mask

    def z_next(self, j, before, here, after):
        base = (j * LANES) % NZ
        straight = here if (base + LANES) % NZ == 0 else jnp.where(self.lane == 0, after, here)
        first = (NZ - 1 - base) % NZ
        wrap = here if first >= NZ - 1 else jnp.where(self.lane >= LANES - (NZ - 1), before, here)
        return jnp.where(self.column(j, NZ - 1), roll(wrap, NZ - 1), roll(straight, -1))

    def z_prev(self, j, before, here, after):
        base = (j * LANES) % NZ
        straight = here if base == 0 else jnp.where(self.lane == LANES - 1, before, here)
        last = LANES - 1 - (base + LANES - 1) % NZ
        wrap = here if last + NZ - 1 < LANES else jnp.where(self.lane < NZ - 1, after, here)
        return jnp.where(self.column(j, 0), roll(wrap, -(NZ - 1)), roll(straight, 1))


def rate(ref, c, x, j, levels, scaled):
    total = None
    for m in range(1, 5):
        ahead = ref[c, x, j, pl.ds(OWN + m, levels), :]
        behind = ref[c, x, j, pl.ds(OWN - m, levels), :]
        term = scaled[m - 1] * (ahead - behind)
        total = term if total is None else total + term
    return total


def fill(scratch, own):
    slabs, levels = own.shape[1], own.shape[2]
    zero = jnp.zeros((levels, LANES), jnp.float32)
    edge = jnp.zeros((4, LANES), jnp.float32)

    def slab(x, carry):
        for c in range(3):
            for j in range(NJ):
                scratch[c, x + 1, j, pl.ds(OWN, levels), :] = own[c, x, :, cols(j)]
                scratch[c, x + 1, j, pl.ds(OWN - 4, 4), :] = edge
                scratch[c, x + 1, j, pl.ds(OWN + levels, 4), :] = edge
        return carry

    lax.fori_loop(0, slabs, slab, 0)
    for c in range(3):
        for j in range(NJ):
            scratch[c, 0, j, pl.ds(OWN, levels), :] = zero
            scratch[c, slabs + 1, j, pl.ds(OWN, levels), :] = zero


class Borders:
    def __init__(self, scaled):
        row = lax.broadcasted_iota(jnp.int32, (8, LANES), 0)
        zero = jnp.zeros((8, LANES), jnp.float32)
        self.low = [jnp.where(row < m, zero - scaled[m - 1], zero) for m in range(1, 5)]
        self.high = [jnp.where(row >= 8 - m, zero + scaled[m - 1], zero) for m in range(1, 5)]
        self.pad = jnp.zeros((4, LANES), jnp.float32)

    def from_low(self, four):
        eight = jnp.concatenate([four, self.pad], axis=0)
        total = self.low[3] * eight
        for m in range(1, 4):
            total = total + self.low[m - 1] * pltpu.roll(eight, m + 4, 0)
        return total

    def from_high(self, four):
        eight = jnp.concatenate([four, self.pad], axis=0)
        total = None
        for m in range(1, 5):
            term = self.high[m - 1] * pltpu.roll(eight, 8 - m, 0)
            total = term if total is None else total + term
        return total


def pack_kernel(own, first, last, down, up):
    levels = own.shape[2]
    x = pl.program_id(0)
    for c in range(3):
        first[c, 0] = own[c, 0, pl.ds(0, 4), :]
        last[c, 0] = own[c, 0, pl.ds(levels - 4, 4), :]

    @pl.when(x == 0)
    def _():
        down[...] = own[:, 0]

    @pl.when(x == pl.num_programs(0) - 1)
    def _():
        up[...] = own[:, 0]


def residual_kernel(spacing, scale, own, forcing, res, rt, grad, scratch):
    levels = own.shape[2]
    x = pl.program_id(0)

    @pl.when(x == 0)
    def _():
        fill(scratch, own)

    scaled = [w * scale[0] for w in weights]
    alpha = 1.0 / (2.0 * spacing)
    beta = viscosity / spacing**2
    sh = Shifts((levels, LANES))

    def at(c, dx, j):
        return scratch[c, x + 1 + dx, j % NJ, pl.ds(OWN, levels), :]

    for j in range(NJ):
        vel = [alpha * at(a, 0, j) for a in range(3)]
        for c in range(3):
            here, before, after = at(c, 0, j), at(c, 0, j - 1), at(c, 0, j + 1)
            pairs = (
                (at(c, 1, j), at(c, -1, j)),
                (sh.y_next(here, after), sh.y_prev(before, here)),
                (sh.z_next(j, before, here, after), sh.z_prev(j, before, here, after)),
            )
            q = rate(scratch, c, x + 1, j, levels, scaled)
            total = q + (6.0 * beta) * here
            near = None
            for a, (nxt, prv) in enumerate(pairs):
                diff = nxt - prv
                grad[a * 3 + c, 0, :, cols(j)] = diff
                total = total + vel[a] * diff
                both = nxt + prv
                near = both if near is None else near + both
            total = total - beta * near
            if c == 0:
                total = total - forcing[:, cols(j)]
            res[c, 0, :, cols(j)] = total
            rt[c, 0, :, cols(j)] = q


def joined_kernel(spacing, scale, part, flow, low, high, left, right, res, first, last, down, up):
    levels = part.shape[2]
    half = levels - 8
    x = pl.program_id(0)
    alpha = 1.0 / (2.0 * spacing)
    beta = viscosity / spacing**2
    border = Borders([w * scale[0] for w in weights])
    for c in range(3):
        for j in range(NJ):
            res[c, 0, pl.ds(0, 8), cols(j)] = part[c, 0, pl.ds(0, 8), cols(j)] + border.from_low(low[c, 0, :, cols(j)])
            res[c, 0, pl.ds(half, 8), cols(j)] = part[c, 0, pl.ds(half, 8), cols(j)] + border.from_high(high[c, 0, :, cols(j)])

    @pl.when(x == 0)
    def _():
        for c in range(3):
            for j in range(NJ):
                plus = alpha * flow[0, 0, :, cols(j)] + beta
                value = res[c, 0, :, cols(j)] - plus * left[c, :, cols(j)]
                res[c, 0, :, cols(j)] = value
                down[c, :, cols(j)] = plus * value

    @pl.when(x == pl.num_programs(0) - 1)
    def _():
        for c in range(3):
            for j in range(NJ):
                minus = alpha * flow[0, 0, :, cols(j)] - beta
                value = res[c, 0, :, cols(j)] + minus * right[c, :, cols(j)]
                res[c, 0, :, cols(j)] = value
                up[c, :, cols(j)] = minus * value

    for c in range(3):
        first[c, 0] = res[c, 0, pl.ds(0, 4), :]
        last[c, 0] = res[c, 0, pl.ds(levels - 4, 4), :]


def descent_kernel(spacing, scale, own, res, left, right, part, grad, low, high, base, rt, sums, scratch, flow, acc):
    levels = own.shape[2]
    slabs = own.shape[1]
    half = levels - 8
    x = pl.program_id(0)
    alpha = 1.0 / (2.0 * spacing)
    beta = viscosity / spacing**2

    @pl.when(x == 0)
    def _():
        fill(scratch, res)
        flow[0] = jnp.zeros_like(flow[0])
        flow[slabs + 1] = jnp.zeros_like(flow[0])

        def slab(i, carry):
            flow[i + 1] = alpha * own[0, i]
            return carry

        lax.fori_loop(0, slabs, slab, 0)
        acc[...] = jnp.zeros_like(acc)

    scaled = [w * scale[0] for w in weights]
    border = Borders(scaled)
    for c in range(3):
        for j in range(NJ):
            rt[c, 0, pl.ds(0, 8), cols(j)] = part[c, 0, pl.ds(0, 8), cols(j)] + border.from_low(low[c, 0, :, cols(j)])
            rt[c, 0, pl.ds(half, 8), cols(j)] = part[c, 0, pl.ds(half, 8), cols(j)] + border.from_high(high[c, 0, :, cols(j)])

    sh = Shifts((levels, LANES))
    is_first = jnp.where(x == 0, 1.0, 0.0).astype(jnp.float32)
    is_last = jnp.where(x == slabs - 1, 1.0, 0.0).astype(jnp.float32)

    def at(c, dx, j):
        return scratch[c, x + 1 + dx, j % NJ, pl.ds(OWN, levels), :]

    s1 = s2 = s3 = None
    for c in range(3):
        cache = {}

        def products(j):
            j = j % NJ
            if j not in cache:
                value = at(c, 0, j)
                y = (alpha * own[1, x, :, cols(j)]) * value
                z = (alpha * own[2, x, :, cols(j)]) * value
                s = beta * value
                cache[j] = (y + s, y - s, z + s, z - s)
            return cache[j]

        for j in range(NJ):
            here = at(c, 0, j)
            (yp0, ym0, zp0, zm0) = products(j - 1)
            (yp1, ym1, zp1, zm1) = products(j)
            (yp2, ym2, zp2, zm2) = products(j + 1)
            total = (6.0 * beta) * here - rate(scratch, c, x + 1, j, levels, scaled)
            nxt, prv = at(c, 1, j), at(c, -1, j)
            total = total - (flow[x + 2, :, cols(j)] + beta) * nxt
            total = total + (flow[x, :, cols(j)] - beta) * prv
            total = total - sh.y_next(yp1, yp2) + sh.y_prev(ym0, ym1)
            total = total - sh.z_next(j, zp0, zp1, zp2) + sh.z_prev(j, zm0, zm1, zm2)
            dots = None
            for k in range(3):
                diff = grad[c * 3 + k, 0, :, cols(j)]
                if c == 0:
                    diff = diff + (is_last * right[k, :, cols(j)] - is_first * left[k, :, cols(j)])
                term = at(k, 0, j) * diff
                dots = term if dots is None else dots + term
            total = total + alpha * dots
            q = rt[c, 0, :, cols(j)]
            t1, t2, t3 = here * q, q * q, total * q
            s1 = t1 if s1 is None else s1 + t1
            s2 = t2 if s2 is None else s2 + t2
            s3 = t3 if s3 is None else s3 + t3
            base[c, 0, :, cols(j)] = own[c, x, :, cols(j)] - step_size * total
    acc[0] += s1
    acc[1] += s2
    acc[2] += s3

    @pl.when(x == slabs - 1)
    def _():
        sums[...] = acc[...]


def closing_kernel(scale, part, rt, low, high, left, right, partial, base, sums, acc):
    levels = part.shape[2]
    half = levels - 8
    x = pl.program_id(0)

    @pl.when(x == 0)
    def _():
        acc[...] = jnp.zeros_like(acc)

    border = Borders([w * scale[0] for w in weights])
    total = jnp.zeros((8, LANES), jnp.float32)
    for c in range(3):
        for j in range(NJ):
            for rows, take in (((0, 8), border.from_low(low[c, 0, :, cols(j)])), ((half, 8), border.from_high(high[c, 0, :, cols(j)]))):
                rows = pl.ds(*rows)
                total = total - take * rt[c, 0, rows, cols(j)]
                base[c, 0, rows, cols(j)] = part[c, 0, rows, cols(j)] + step_size * take
    acc[...] += total

    def edge(sign, message):
        total = jnp.zeros((levels, LANES), jnp.float32)
        for c in range(3):
            for j in range(NJ):
                extra = message[c, :, cols(j)]
                total = total + extra * rt[c, 0, :, cols(j)]
                base[c, 0, :, cols(j)] = base[c, 0, :, cols(j)] - (sign * step_size) * extra
        acc[...] += sign * (total[:8] + total[half:])

    @pl.when(x == 0)
    def _():
        edge(1.0, left)

    @pl.when(x == pl.num_programs(0) - 1)
    def _():
        edge(-1.0, right)
        lane = lax.broadcasted_iota(jnp.int32, (1, LANES), 1)
        row = jnp.zeros((1, LANES), jnp.float32)
        for k in range(3):
            value = jnp.sum(partial[k]) if k < 2 else jnp.sum(partial[k]) + jnp.sum(acc[...])
            row = jnp.where(lane == k, value, row)
        sums[...] = jnp.broadcast_to(row[None], sums.shape)


def update_kernel(cells, period, gathered, base, rt, out, pgrad, weight):
    @pl.when(pl.program_id(0) == 0)
    def _():
        row = jnp.sum(gathered[...], axis=0)
        s1, s2, s3 = row[0, 0], row[0, 1], row[0, 2]
        ratio = jnp.full((1, LANES), step_size * s3, jnp.float32) / jnp.full((1, LANES), s2, jnp.float32)
        weight[...] = jnp.broadcast_to(ratio, weight.shape)
        pgrad[...] = jnp.full((1, LANES), -s1, jnp.float32) / jnp.full((1, LANES), period[0] * cells, jnp.float32)

    factor = weight[...]
    levels = base.shape[2]
    for c in range(3):
        for j in range(NJ):
            for row in range(0, levels, 8):
                rows = pl.ds(row, 8)
                out[c, 0, rows, cols(j)] = base[c, 0, rows, cols(j)] + factor * rt[c, 0, rows, cols(j)]


def ring(axis):
    count = lax.axis_size(axis)
    up = [(i, (i + 1) % count) for i in range(count)]
    return up, [(j, i) for i, j in up]


def exchange(first, last, down, up):
    tm_up, tm_down = ring(TM)
    space_up, space_down = ring(SPACE)
    left = lax.ppermute(up, SPACE, space_up)
    right = lax.ppermute(down, SPACE, space_down)
    low = lax.ppermute(last, TM, tm_up)
    high = lax.ppermute(first, TM, tm_down)
    return low, high, left, right


def on_device(velocity, period, wavenumber):
    levels, _, slabs, _ = velocity.shape
    devices = lax.axis_size(ALL)
    total_levels = levels * lax.axis_size(TM)
    grid_first = slabs * lax.axis_size(SPACE)
    spacing = 2.0 * math.pi / NY
    u = jnp.transpose(velocity, (1, 2, 0, 3))
    scale = total_levels / period
    row_index = jnp.arange(NY, dtype=jnp.float32)
    profile = jnp.sin(wavenumber[0].astype(jnp.float32) * (2.0 * math.pi / NY) * row_index)
    forcing = jnp.repeat(profile, NZ).reshape(1, NC)

    vmem = pl.BlockSpec(memory_space=pltpu.VMEM)
    smem = pl.BlockSpec(memory_space=pltpu.SMEM)
    slab1 = pl.BlockSpec((1, 1, levels, NC), lambda i: (0, i, 0, 0))
    slab3 = pl.BlockSpec((3, 1, levels, NC), lambda i: (0, i, 0, 0))
    slab9 = pl.BlockSpec((9, 1, levels, NC), lambda i: (0, i, 0, 0))
    four3 = pl.BlockSpec((3, 1, 4, NC), lambda i: (0, i, 0, 0))
    edge3 = pl.BlockSpec((3, levels, NC), lambda i: (0, 0, 0))
    sums3 = pl.BlockSpec((3, levels, LANES), lambda i: (0, 0, 0))

    def shape(*dims):
        return jax.ShapeDtypeStruct(dims, jnp.float32)

    field = shape(3, slabs, levels, NC)
    four = shape(3, slabs, 4, NC)
    edge = shape(3, levels, NC)
    padded = pltpu.VMEM((3, slabs + 2, NJ, ROWS, LANES), jnp.float32)
    work = pl.CostEstimate(flops=30_000_000, bytes_accessed=40_000_000, transcendentals=0)
    little = pl.CostEstimate(flops=3_000_000, bytes_accessed=6_000_000, transcendentals=0)

    first, last, down, up = pl.pallas_call(
        pack_kernel,
        grid=(slabs,),
        in_specs=[slab3],
        out_specs=[four3, four3, edge3, edge3],
        out_shape=[four, four, edge, edge],
        cost_estimate=little,
        name="pack",
    )(u)
    low, high, left, right = exchange(first, last, down, up)
    res_part, rt_part, grad = pl.pallas_call(
        lambda *refs: residual_kernel(spacing, *refs),
        grid=(slabs,),
        in_specs=[smem, vmem, vmem],
        out_specs=[slab3, slab3, slab9],
        out_shape=[field, field, shape(9, slabs, levels, NC)],
        scratch_shapes=[padded],
        cost_estimate=work,
        name="residual",
    )(scale, u, forcing)

    res, first, last, down, up = pl.pallas_call(
        lambda *refs: joined_kernel(spacing, *refs),
        grid=(slabs,),
        in_specs=[smem, slab3, slab1, four3, four3, vmem, vmem],
        out_specs=[slab3, four3, four3, edge3, edge3],
        out_shape=[field, four, four, edge, edge],
        cost_estimate=little,
        name="joined",
    )(scale, res_part, u, low, high, left, right)
    res_low, res_high, res_left, res_right = exchange(first, last, down, up)
    base_part, rt, partial = pl.pallas_call(
        lambda *refs: descent_kernel(spacing, *refs),
        grid=(slabs,),
        in_specs=[smem, vmem, vmem, vmem, vmem, slab3, slab9, four3, four3],
        out_specs=[slab3, slab3, sums3],
        out_shape=[field, field, shape(3, levels, LANES)],
        scratch_shapes=[
            padded,
            pltpu.VMEM((slabs + 2, levels, NC), jnp.float32),
            pltpu.VMEM((3, levels, LANES), jnp.float32),
        ],
        cost_estimate=work,
        name="descent",
    )(scale, u, res, left, right, rt_part, grad, low, high)
    base, sums = pl.pallas_call(
        closing_kernel,
        grid=(slabs,),
        in_specs=[smem, slab3, slab3, four3, four3, vmem, vmem, vmem],
        out_specs=[slab3, pl.BlockSpec((devices, 1, LANES), lambda i: (0, 0, 0))],
        out_shape=[field, shape(devices, 1, LANES)],
        scratch_shapes=[pltpu.VMEM((8, LANES), jnp.float32)],
        cost_estimate=little,
        name="closing",
    )(scale, base_part, rt, res_low, res_high, res_left, res_right, partial)

    gathered = lax.all_to_all(sums, ALL, 0, 0)
    cells = 3.0 * total_levels * grid_first * NY * NZ
    updated, pgrad = pl.pallas_call(
        lambda *refs: update_kernel(cells, *refs),
        grid=(slabs,),
        in_specs=[smem, vmem, slab3, slab3],
        out_specs=[slab3, pl.BlockSpec((1, LANES), lambda i: (0, 0))],
        out_shape=[field, shape(1, LANES)],
        scratch_shapes=[pltpu.VMEM((8, LANES), jnp.float32)],
        cost_estimate=little,
        name="update",
    )(period, gathered, base, rt)
    back = (2, 0, 1, 3)
    return jnp.transpose(updated, back), jnp.transpose(res, back), pgrad[0, :1]


def solution(mesh):
    split = Mesh(mesh.devices.reshape(2, 4, 2, 2, 4), ALL)
    in_specs = (P(TM, None, SPACE, None), P(), P())
    out_specs = (P(TM, None, SPACE, None), P(TM, None, SPACE, None), P())
    return jax.shard_map(on_device, mesh=split, in_specs=in_specs, out_specs=out_specs, check_vma=False)
```

```python
import math

import jax
import jax.numpy as jnp
from jax import lax
from jax.experimental import pallas as pl
from jax.experimental.pallas import tpu as pltpu
from jax.sharding import Mesh
from jax.sharding import PartitionSpec as P

NY = 48
NZ = 48
NC = NY * NZ
LANES = 128
NJ = NC // LANES
TM = ("tm_0", "tm_1", "tm_2")
SPACE = ("space_0", "space_1")
ALL = TM + SPACE

weights = (0.8, -0.2, 4.0 / 105.0, -1.0 / 280.0)
viscosity = 0.02
step_size = 0.15

ROWS = 32
OWN = 8


def cols(j):
    return pl.ds(j * LANES, LANES)


def roll(x, shift):
    return pltpu.roll(x, shift % LANES, x.ndim - 1)


class Shifts:
    def __init__(self, shape):
        self.lane = lax.broadcasted_iota(jnp.int32, shape, len(shape) - 1)

    def y_next(self, here, after):
        return roll(jnp.where(self.lane < NZ, after, here), -NZ)

    def y_prev(self, before, here):
        return roll(jnp.where(self.lane >= LANES - NZ, before, here), NZ)

    def column(self, j, value):
        base = (j * LANES) % NZ
        mask = None
        for lane in range(LANES):
            if (base + lane) % NZ == value:
                one = self.lane == lane
                mask = one if mask is None else jnp.logical_or(mask, one)
        return mask

    def z_next(self, j, before, here, after):
        base = (j * LANES) % NZ
        straight = here if (base + LANES) % NZ == 0 else jnp.where(self.lane == 0, after, here)
        first = (NZ - 1 - base) % NZ
        wrap = here if first >= NZ - 1 else jnp.where(self.lane >= LANES - (NZ - 1), before, here)
        return jnp.where(self.column(j, NZ - 1), roll(wrap, NZ - 1), roll(straight, -1))

    def z_prev(self, j, before, here, after):
        base = (j * LANES) % NZ
        straight = here if base == 0 else jnp.where(self.lane == LANES - 1, before, here)
        last = LANES - 1 - (base + LANES - 1) % NZ
        wrap = here if last + NZ - 1 < LANES else jnp.where(self.lane < NZ - 1, after, here)
        return jnp.where(self.column(j, 0), roll(wrap, -(NZ - 1)), roll(straight, 1))


def rate(ref, c, x, j, levels, scaled):
    total = None
    for m in range(1, 5):
        ahead = ref[c, x, j, pl.ds(OWN + m, levels), :]
        behind = ref[c, x, j, pl.ds(OWN - m, levels), :]
        term = scaled[m - 1] * (ahead - behind)
        total = term if total is None else total + term
    return total


def fill(scratch, own):
    slabs, levels = own.shape[1], own.shape[2]
    zero = jnp.zeros((levels, LANES), jnp.float32)
    edge = jnp.zeros((4, LANES), jnp.float32)

    def slab(x, carry):
        for c in range(3):
            for j in range(NJ):
                scratch[c, x + 1, j, pl.ds(OWN, levels), :] = own[c, x, :, cols(j)]
                scratch[c, x + 1, j, pl.ds(OWN - 4, 4), :] = edge
                scratch[c, x + 1, j, pl.ds(OWN + levels, 4), :] = edge
        return carry

    lax.fori_loop(0, slabs, slab, 0)
    for c in range(3):
        for j in range(NJ):
            scratch[c, 0, j, pl.ds(OWN, levels), :] = zero
            scratch[c, slabs + 1, j, pl.ds(OWN, levels), :] = zero


class Borders:
    def __init__(self, scaled):
        row = lax.broadcasted_iota(jnp.int32, (8, LANES), 0) % 4
        zero = jnp.zeros((8, LANES), jnp.float32)
        self.low = [jnp.where(row < m, zero - scaled[m - 1], zero) for m in range(1, 5)]
        self.high = [jnp.where(row >= 4 - m, zero + scaled[m - 1], zero) for m in range(1, 5)]

    def pair(self, coefficients, sign, message, c, x, j):
        eight = jnp.concatenate([message[c, x, :, cols(j)], message[c, x, :, cols(j + 1)]], axis=0)
        total = coefficients[3] * eight
        for m in range(1, 4):
            total = total + coefficients[m - 1] * pltpu.roll(eight, (sign * (4 - m)) % 8, 0)
        return total[:4], total[4:]

    def from_low(self, message, c, x, j):
        return self.pair(self.low, -1, message, c, x, j)

    def from_high(self, message, c, x, j):
        return self.pair(self.high, 1, message, c, x, j)


def add_borders(border, ref, low, high, c, x, levels):
    for j in range(0, NJ, 2):
        below, above = border.from_low(low, c, x, j), border.from_high(high, c, x, j)
        for k in range(2):
            ref[c, x, pl.ds(0, 4), cols(j + k)] += below[k]
            ref[c, x, pl.ds(levels - 4, 4), cols(j + k)] += above[k]


def pack_kernel(own, first, last, down, up, first_buffer, last_buffer, sems):
    slabs, levels = own.shape[1], own.shape[2]
    copies = [
        pltpu.make_async_copy(own.at[:, 0], down, sems.at[0]),
        pltpu.make_async_copy(own.at[:, slabs - 1], up, sems.at[1]),
    ]
    for copy in copies:
        copy.start()
    first_buffer[...] = own[:, :, pl.ds(0, 4), :]
    last_buffer[...] = own[:, :, pl.ds(levels - 4, 4), :]
    copies += [
        pltpu.make_async_copy(first_buffer, first, sems.at[2]),
        pltpu.make_async_copy(last_buffer, last, sems.at[3]),
    ]
    for copy in copies[2:]:
        copy.start()
    for copy in copies:
        copy.wait()


def residual_kernel(spacing, scale, own, forcing, res, rt, grad, scratch):
    levels = own.shape[2]
    x = pl.program_id(0)

    @pl.when(x == 0)
    def _():
        fill(scratch, own)

    scaled = [w * scale[0] for w in weights]
    alpha = 1.0 / (2.0 * spacing)
    beta = viscosity / spacing**2
    sh = Shifts((levels, LANES))

    def at(c, dx, j):
        return scratch[c, x + 1 + dx, j % NJ, pl.ds(OWN, levels), :]

    for j in range(NJ):
        vel = [alpha * at(a, 0, j) for a in range(3)]
        for c in range(3):
            here, before, after = at(c, 0, j), at(c, 0, j - 1), at(c, 0, j + 1)
            pairs = (
                (at(c, 1, j), at(c, -1, j)),
                (sh.y_next(here, after), sh.y_prev(before, here)),
                (sh.z_next(j, before, here, after), sh.z_prev(j, before, here, after)),
            )
            q = rate(scratch, c, x + 1, j, levels, scaled)
            total = q + (6.0 * beta) * here
            near = None
            for a, (nxt, prv) in enumerate(pairs):
                diff = nxt - prv
                grad[a * 3 + c, 0, :, cols(j)] = diff
                total = total + vel[a] * diff
                both = nxt + prv
                near = both if near is None else near + both
            total = total - beta * near
            if c == 0:
                total = total - forcing[:, cols(j)]
            res[c, 0, :, cols(j)] = total
            rt[c, 0, :, cols(j)] = q


def joined_kernel(spacing, scale, part, own, low, high, left, right, res, first, last, down, up, first_buffer, last_buffer, down_buffer, up_buffer, sems):
    slabs, levels = own.shape[1], own.shape[2]
    alpha = 1.0 / (2.0 * spacing)
    beta = viscosity / spacing**2
    border = Borders([w * scale[0] for w in weights])

    def slab(x):
        for c in range(3):
            res[c, x] = part[c, x]
            add_borders(border, res, low, high, c, x, levels)

    slab(0)
    for c in range(3):
        for j in range(NJ):
            plus = alpha * own[0, 0, :, cols(j)] + beta
            value = res[c, 0, :, cols(j)] - plus * left[c, :, cols(j)]
            res[c, 0, :, cols(j)] = value
            down_buffer[c, :, cols(j)] = plus * value
    copies = [pltpu.make_async_copy(down_buffer, down, sems.at[0])]
    copies[0].start()

    slab(slabs - 1)
    for c in range(3):
        for j in range(NJ):
            minus = alpha * own[0, slabs - 1, :, cols(j)] - beta
            value = res[c, slabs - 1, :, cols(j)] + minus * right[c, :, cols(j)]
            res[c, slabs - 1, :, cols(j)] = value
            up_buffer[c, :, cols(j)] = minus * value
    copies += [pltpu.make_async_copy(up_buffer, up, sems.at[1])]
    copies[1].start()

    def inner(x, carry):
        slab(x)
        return carry

    lax.fori_loop(1, slabs - 1, inner, 0)
    first_buffer[...] = res[:, :, pl.ds(0, 4), :]
    last_buffer[...] = res[:, :, pl.ds(levels - 4, 4), :]
    copies += [
        pltpu.make_async_copy(first_buffer, first, sems.at[2]),
        pltpu.make_async_copy(last_buffer, last, sems.at[3]),
    ]
    for copy in copies[2:]:
        copy.start()
    for copy in copies:
        copy.wait()


def descent_kernel(spacing, scale, own, res, left, right, part, grad, low, high, base, rt, sums, scratch, flow, acc):
    levels = own.shape[2]
    slabs = own.shape[1]
    x = pl.program_id(0)
    alpha = 1.0 / (2.0 * spacing)
    beta = viscosity / spacing**2

    @pl.when(x == 0)
    def _():
        fill(scratch, res)
        flow[0] = jnp.zeros_like(flow[0])
        flow[slabs + 1] = jnp.zeros_like(flow[0])

        def slab(i, carry):
            flow[i + 1] = alpha * own[0, i]
            return carry

        lax.fori_loop(0, slabs, slab, 0)
        acc[...] = jnp.zeros_like(acc)

    scaled = [w * scale[0] for w in weights]
    border = Borders(scaled)
    rt[...] = part[...]
    for c in range(3):
        add_borders(border, rt, low, high, c, 0, levels)

    sh = Shifts((levels, LANES))
    is_first = jnp.where(x == 0, 1.0, 0.0).astype(jnp.float32)
    is_last = jnp.where(x == slabs - 1, 1.0, 0.0).astype(jnp.float32)

    def at(c, dx, j):
        return scratch[c, x + 1 + dx, j % NJ, pl.ds(OWN, levels), :]

    s1 = s2 = s3 = None
    for c in range(3):
        cache = {}

        def products(j):
            j = j % NJ
            if j not in cache:
                value = at(c, 0, j)
                y = (alpha * own[1, x, :, cols(j)]) * value
                z = (alpha * own[2, x, :, cols(j)]) * value
                s = beta * value
                cache[j] = (y + s, y - s, z + s, z - s)
            return cache[j]

        for j in range(NJ):
            here = at(c, 0, j)
            (yp0, ym0, zp0, zm0) = products(j - 1)
            (yp1, ym1, zp1, zm1) = products(j)
            (yp2, ym2, zp2, zm2) = products(j + 1)
            total = (6.0 * beta) * here - rate(scratch, c, x + 1, j, levels, scaled)
            nxt, prv = at(c, 1, j), at(c, -1, j)
            total = total - (flow[x + 2, :, cols(j)] + beta) * nxt
            total = total + (flow[x, :, cols(j)] - beta) * prv
            total = total - sh.y_next(yp1, yp2) + sh.y_prev(ym0, ym1)
            total = total - sh.z_next(j, zp0, zp1, zp2) + sh.z_prev(j, zm0, zm1, zm2)
            dots = None
            for k in range(3):
                diff = grad[c * 3 + k, 0, :, cols(j)]
                if c == 0:
                    diff = diff + (is_last * right[k, :, cols(j)] - is_first * left[k, :, cols(j)])
                term = at(k, 0, j) * diff
                dots = term if dots is None else dots + term
            total = total + alpha * dots
            q = rt[c, 0, :, cols(j)]
            t1, t2, t3 = here * q, q * q, total * q
            s1 = t1 if s1 is None else s1 + t1
            s2 = t2 if s2 is None else s2 + t2
            s3 = t3 if s3 is None else s3 + t3
            base[c, 0, :, cols(j)] = own[c, x, :, cols(j)] - step_size * total
    acc[0] += s1
    acc[1] += s2
    acc[2] += s3

    @pl.when(x == slabs - 1)
    def _():
        sums[...] = acc[...]


def closing_kernel(scale, part, rt, low, high, left, right, partial, base, sums):
    slabs, levels = part.shape[1], part.shape[2]
    border = Borders([w * scale[0] for w in weights])

    def slab(x, total):
        for c in range(3):
            base[c, x] = part[c, x]
            for j in range(0, NJ, 2):
                below, above = border.from_low(low, c, x, j), border.from_high(high, c, x, j)
                for k in range(2):
                    for row, take in ((0, below[k]), (levels - 4, above[k])):
                        rows = pl.ds(row, 4)
                        total = total - take * rt[c, x, rows, cols(j + k)]
                        base[c, x, rows, cols(j + k)] += step_size * take
        return total

    inner = lax.fori_loop(0, slabs, slab, jnp.zeros((4, LANES), jnp.float32))

    def edge(sign, message, x):
        total = jnp.zeros((levels, LANES), jnp.float32)
        for c in range(3):
            for j in range(NJ):
                extra = message[c, :, cols(j)]
                total = total + extra * rt[c, x, :, cols(j)]
                base[c, x, :, cols(j)] = base[c, x, :, cols(j)] - (sign * step_size) * extra
        return sign * total

    outer = edge(1.0, left, 0) + edge(-1.0, right, slabs - 1)
    lane = lax.broadcasted_iota(jnp.int32, (1, LANES), 1)
    row = jnp.zeros((1, LANES), jnp.float32)
    for k in range(3):
        value = jnp.sum(partial[k]) if k < 2 else jnp.sum(partial[k] + outer) + jnp.sum(inner)
        row = jnp.where(lane == k, value, row)
    sums[...] = jnp.broadcast_to(row[None], sums.shape)


def update_kernel(cells, period, gathered, base, rt, out, pgrad, buffer, sem):
    slabs, levels = base.shape[1], base.shape[2]
    row = jnp.sum(gathered[...], axis=0)
    s1, s2, s3 = row[0, 0], row[0, 1], row[0, 2]
    ratio = jnp.full((1, LANES), step_size * s3, jnp.float32) / jnp.full((1, LANES), s2, jnp.float32)
    factor = jnp.broadcast_to(ratio, (levels, LANES))
    pgrad[...] = jnp.full((1, LANES), -s1, jnp.float32) / jnp.full((1, LANES), period[0] * cells, jnp.float32)

    def slab(x, carry):
        for c in range(3):
            for j in range(NJ):
                buffer[c, x, :, cols(j)] = base[c, x, :, cols(j)] + factor * rt[c, x, :, cols(j)]
        pltpu.make_async_copy(buffer.at[:, x], out.at[:, x], sem).start()
        return carry

    lax.fori_loop(0, slabs, slab, 0)
    pltpu.make_async_copy(buffer, out, sem).wait()


def ring(axis):
    count = lax.axis_size(axis)
    up = [(i, (i + 1) % count) for i in range(count)]
    return up, [(j, i) for i, j in up]


def exchange(first, last, down, up):
    tm_up, tm_down = ring(TM)
    space_up, space_down = ring(SPACE)
    left = lax.ppermute(up, SPACE, space_up)
    right = lax.ppermute(down, SPACE, space_down)
    low = lax.ppermute(last, TM, tm_up)
    high = lax.ppermute(first, TM, tm_down)
    return low, high, left, right


def on_device(velocity, period, wavenumber):
    levels, _, slabs, _ = velocity.shape
    devices = lax.axis_size(ALL)
    total_levels = levels * lax.axis_size(TM)
    grid_first = slabs * lax.axis_size(SPACE)
    spacing = 2.0 * math.pi / NY
    u = jnp.transpose(velocity, (1, 2, 0, 3))
    scale = total_levels / period
    row_index = jnp.arange(NY, dtype=jnp.float32)
    profile = jnp.sin(wavenumber[0].astype(jnp.float32) * (2.0 * math.pi / NY) * row_index)
    forcing = jnp.repeat(profile, NZ).reshape(1, NC)

    vmem = pl.BlockSpec(memory_space=pltpu.VMEM)
    smem = pl.BlockSpec(memory_space=pltpu.SMEM)
    hbm = pl.BlockSpec(memory_space=pl.ANY)
    slab3 = pl.BlockSpec((3, 1, levels, NC), lambda i: (0, i, 0, 0))
    slab9 = pl.BlockSpec((9, 1, levels, NC), lambda i: (0, i, 0, 0))
    four3 = pl.BlockSpec((3, 1, 4, NC), lambda i: (0, i, 0, 0))
    sums3 = pl.BlockSpec((3, levels, LANES), lambda i: (0, 0, 0))

    def shape(*dims):
        return jax.ShapeDtypeStruct(dims, jnp.float32)

    def params(mib):
        return pltpu.CompilerParams(vmem_limit_bytes=mib << 20)

    field = shape(3, slabs, levels, NC)
    four = shape(3, slabs, 4, NC)
    edge = shape(3, levels, NC)
    four_buffer = pltpu.VMEM((3, slabs, 4, NC), jnp.float32)
    edge_buffer = pltpu.VMEM((3, levels, NC), jnp.float32)
    padded = pltpu.VMEM((3, slabs + 2, NJ, ROWS, LANES), jnp.float32)
    work = pl.CostEstimate(flops=30_000_000, bytes_accessed=40_000_000, transcendentals=0)
    little = pl.CostEstimate(flops=3_000_000, bytes_accessed=6_000_000, transcendentals=0)

    first, last, down, up = pl.pallas_call(
        pack_kernel,
        in_specs=[vmem],
        out_specs=[hbm] * 4,
        out_shape=[four, four, edge, edge],
        scratch_shapes=[four_buffer, four_buffer, pltpu.SemaphoreType.DMA((4,))],
        compiler_params=params(8),
        cost_estimate=little,
        name="pack",
    )(u)
    low, high, left, right = exchange(first, last, down, up)
    res_part, rt_part, grad = pl.pallas_call(
        lambda *refs: residual_kernel(spacing, *refs),
        grid=(slabs,),
        in_specs=[smem, vmem, vmem],
        out_specs=[slab3, slab3, slab9],
        out_shape=[field, field, shape(9, slabs, levels, NC)],
        scratch_shapes=[padded],
        compiler_params=params(20),
        cost_estimate=work,
        name="residual",
    )(scale, u, forcing)

    res, first, last, down, up = pl.pallas_call(
        lambda *refs: joined_kernel(spacing, *refs),
        in_specs=[smem] + [vmem] * 6,
        out_specs=[vmem] + [hbm] * 4,
        out_shape=[field, four, four, edge, edge],
        scratch_shapes=[four_buffer, four_buffer, edge_buffer, edge_buffer, pltpu.SemaphoreType.DMA((4,))],
        compiler_params=params(18),
        cost_estimate=little,
        name="joined",
    )(scale, res_part, u, low, high, left, right)
    res_low, res_high, res_left, res_right = exchange(first, last, down, up)
    base_part, rt, partial = pl.pallas_call(
        lambda *refs: descent_kernel(spacing, *refs),
        grid=(slabs,),
        in_specs=[smem, vmem, vmem, vmem, vmem, slab3, slab9, four3, four3],
        out_specs=[slab3, slab3, sums3],
        out_shape=[field, field, shape(3, levels, LANES)],
        scratch_shapes=[
            padded,
            pltpu.VMEM((slabs + 2, levels, NC), jnp.float32),
            pltpu.VMEM((3, levels, LANES), jnp.float32),
        ],
        compiler_params=params(26),
        cost_estimate=work,
        name="descent",
    )(scale, u, res, left, right, rt_part, grad, low, high)
    base, sums = pl.pallas_call(
        closing_kernel,
        in_specs=[smem] + [vmem] * 7,
        out_specs=[vmem, vmem],
        out_shape=[field, shape(devices, 1, LANES)],
        compiler_params=params(16),
        cost_estimate=little,
        name="closing",
    )(scale, base_part, rt, res_low, res_high, res_left, res_right, partial)

    gathered = lax.all_to_all(sums, ALL, 0, 0)
    cells = 3.0 * total_levels * grid_first * NY * NZ
    updated, pgrad = pl.pallas_call(
        lambda *refs: update_kernel(cells, *refs),
        in_specs=[smem, vmem, vmem, vmem],
        out_specs=[hbm, vmem],
        out_shape=[field, shape(1, LANES)],
        scratch_shapes=[pltpu.VMEM((3, slabs, levels, NC), jnp.float32), pltpu.SemaphoreType.DMA],
        compiler_params=params(14),
        cost_estimate=little,
        name="update",
    )(period, gathered, base, rt)
    back = (2, 0, 1, 3)
    return jnp.transpose(updated, back), jnp.transpose(res, back), pgrad[0, :1]


def solution(mesh):
    split = Mesh(mesh.devices.reshape(2, 4, 2, 2, 4), ALL)
    in_specs = (P(TM, None, SPACE, None), P(), P())
    out_specs = (P(TM, None, SPACE, None), P(TM, None, SPACE, None), P())
    return jax.shard_map(on_device, mesh=split, in_specs=in_specs, out_specs=out_specs, check_vma=False)
```

```python
import math

import jax
import jax.numpy as jnp
from jax import lax
from jax.experimental import pallas as pl
from jax.experimental.pallas import tpu as pltpu
from jax.sharding import Mesh
from jax.sharding import PartitionSpec as P


NY = 48
NZ = 48
NC = NY * NZ
LANES = 128
NJ = NC // LANES
TM = ("tm_0", "tm_1", "tm_2")
SPACE = ("space_0", "space_1")
ALL = TM + SPACE

weights = (0.8, -0.2, 4.0 / 105.0, -1.0 / 280.0)
viscosity = 0.02
step_size = 0.15

ROWS = 32
OWN = 8


def cols(j):
    return pl.ds(j * LANES, LANES)


def roll(x, shift):
    return pltpu.roll(x, shift % LANES, x.ndim - 1)


class Shifts:
    def __init__(self, shape):
        self.lane = lax.broadcasted_iota(jnp.int32, shape, len(shape) - 1)

    def y_next(self, here, after):
        return roll(jnp.where(self.lane < NZ, after, here), -NZ)

    def y_prev(self, before, here):
        return roll(jnp.where(self.lane >= LANES - NZ, before, here), NZ)

    def column(self, j, value):
        base = (j * LANES) % NZ
        mask = None
        for lane in range(LANES):
            if (base + lane) % NZ == value:
                one = self.lane == lane
                mask = one if mask is None else jnp.logical_or(mask, one)
        return mask

    def z_next(self, j, before, here, after):
        base = (j * LANES) % NZ
        straight = here if (base + LANES) % NZ == 0 else jnp.where(self.lane == 0, after, here)
        first = (NZ - 1 - base) % NZ
        wrap = here if first >= NZ - 1 else jnp.where(self.lane >= LANES - (NZ - 1), before, here)
        return jnp.where(self.column(j, NZ - 1), roll(wrap, NZ - 1), roll(straight, -1))

    def z_prev(self, j, before, here, after):
        base = (j * LANES) % NZ
        straight = here if base == 0 else jnp.where(self.lane == LANES - 1, before, here)
        last = LANES - 1 - (base + LANES - 1) % NZ
        wrap = here if last + NZ - 1 < LANES else jnp.where(self.lane < NZ - 1, after, here)
        return jnp.where(self.column(j, 0), roll(wrap, -(NZ - 1)), roll(straight, 1))


def rate(ref, c, x, j, levels, scaled):
    total = None
    for m in range(1, 5):
        ahead = ref[c, x, j, pl.ds(OWN + m, levels), :]
        behind = ref[c, x, j, pl.ds(OWN - m, levels), :]
        term = scaled[m - 1] * (ahead - behind)
        total = term if total is None else total + term
    return total


def fill(scratch, own):
    slabs, levels = own.shape[1], own.shape[2]
    zero = jnp.zeros((levels, LANES), jnp.float32)
    edge = jnp.zeros((4, LANES), jnp.float32)

    def slab(x, carry):
        for c in range(3):
            for j in range(NJ):
                scratch[c, x + 1, j, pl.ds(OWN, levels), :] = own[c, x, :, cols(j)]
                scratch[c, x + 1, j, pl.ds(OWN - 4, 4), :] = edge
                scratch[c, x + 1, j, pl.ds(OWN + levels, 4), :] = edge
        return carry

    lax.fori_loop(0, slabs, slab, 0)
    for c in range(3):
        for j in range(NJ):
            scratch[c, 0, j, pl.ds(OWN, levels), :] = zero
            scratch[c, slabs + 1, j, pl.ds(OWN, levels), :] = zero


class Borders:
    def __init__(self, scaled):
        row = lax.broadcasted_iota(jnp.int32, (8, LANES), 0) % 4
        zero = jnp.zeros((8, LANES), jnp.float32)
        self.low = [jnp.where(row < m, zero - scaled[m - 1], zero) for m in range(1, 5)]
        self.high = [jnp.where(row >= 4 - m, zero + scaled[m - 1], zero) for m in range(1, 5)]

    def pair(self, coefficients, sign, message, c, x, j):
        eight = jnp.concatenate([message[c, x, :, cols(j)], message[c, x, :, cols(j + 1)]], axis=0)
        total = coefficients[3] * eight
        for m in range(1, 4):
            total = total + coefficients[m - 1] * pltpu.roll(eight, (sign * (4 - m)) % 8, 0)
        return total[:4], total[4:]

    def from_low(self, message, c, x, j):
        return self.pair(self.low, -1, message, c, x, j)

    def from_high(self, message, c, x, j):
        return self.pair(self.high, 1, message, c, x, j)


def add_borders(border, ref, low, high, c, x, levels):
    for j in range(0, NJ, 2):
        below, above = border.from_low(low, c, x, j), border.from_high(high, c, x, j)
        for k in range(2):
            ref[c, x, pl.ds(0, 4), cols(j + k)] += below[k]
            ref[c, x, pl.ds(levels - 4, 4), cols(j + k)] += above[k]


def edges_kernel(own, down, up, sems):
    slabs = own.shape[1]
    copies = [
        pltpu.make_async_copy(own.at[:, slabs - 1], up, sems.at[0]),
        pltpu.make_async_copy(own.at[:, 0], down, sems.at[1]),
    ]
    for copy in copies:
        copy.start()
    for copy in copies:
        copy.wait()


def ends_kernel(own, first, last):
    levels = own.shape[2]
    first[...] = own[:, :, pl.ds(0, 4), :]
    last[...] = own[:, :, pl.ds(levels - 4, 4), :]


def residual_kernel(spacing, scale, own, forcing, res, rt, grad, scratch):
    levels = own.shape[2]
    x = pl.program_id(0)

    @pl.when(x == 0)
    def _():
        fill(scratch, own)

    scaled = [w * scale[0] for w in weights]
    alpha = 1.0 / (2.0 * spacing)
    beta = viscosity / spacing**2
    sh = Shifts((levels, LANES))

    def at(c, dx, j):
        return scratch[c, x + 1 + dx, j % NJ, pl.ds(OWN, levels), :]

    for j in range(NJ):
        vel = [alpha * at(a, 0, j) for a in range(3)]
        for c in range(3):
            here, before, after = at(c, 0, j), at(c, 0, j - 1), at(c, 0, j + 1)
            pairs = (
                (at(c, 1, j), at(c, -1, j)),
                (sh.y_next(here, after), sh.y_prev(before, here)),
                (sh.z_next(j, before, here, after), sh.z_prev(j, before, here, after)),
            )
            q = rate(scratch, c, x + 1, j, levels, scaled)
            total = q + (6.0 * beta) * here
            near = None
            for a, (nxt, prv) in enumerate(pairs):
                diff = nxt - prv
                grad[a * 3 + c, 0, :, cols(j)] = diff
                total = total + vel[a] * diff
                both = nxt + prv
                near = both if near is None else near + both
            total = total - beta * near
            if c == 0:
                total = total - forcing[:, cols(j)]
            res[c, 0, :, cols(j)] = total
            rt[c, 0, :, cols(j)] = q


def joined_kernel(spacing, scale, part, own, low, high, left, right, res, first, last, down, up):
    slabs, levels = own.shape[1], own.shape[2]
    alpha = 1.0 / (2.0 * spacing)
    beta = viscosity / spacing**2
    border = Borders([w * scale[0] for w in weights])

    def slab(x, carry):
        for c in range(3):
            res[c, x] = part[c, x]
            add_borders(border, res, low, high, c, x, levels)
        return carry

    lax.fori_loop(0, slabs, slab, 0)
    for c in range(3):
        for j in range(NJ):
            plus = alpha * own[0, 0, :, cols(j)] + beta
            value = res[c, 0, :, cols(j)] - plus * left[c, :, cols(j)]
            res[c, 0, :, cols(j)] = value
            down[c, :, cols(j)] = plus * value
            minus = alpha * own[0, slabs - 1, :, cols(j)] - beta
            value = res[c, slabs - 1, :, cols(j)] + minus * right[c, :, cols(j)]
            res[c, slabs - 1, :, cols(j)] = value
            up[c, :, cols(j)] = minus * value
    first[...] = res[:, :, pl.ds(0, 4), :]
    last[...] = res[:, :, pl.ds(levels - 4, 4), :]


def descent_kernel(spacing, scale, own, res, left, right, part, grad, low, high, base, rt, sums, res_out, scratch, flow, acc, sem):
    levels = own.shape[2]
    slabs = own.shape[1]
    x = pl.program_id(0)
    alpha = 1.0 / (2.0 * spacing)
    beta = viscosity / spacing**2

    @pl.when(x == 0)
    def _():
        pltpu.make_async_copy(res, res_out, sem).start()
        fill(scratch, res)
        flow[0] = jnp.zeros_like(flow[0])
        flow[slabs + 1] = jnp.zeros_like(flow[0])

        def slab(i, carry):
            flow[i + 1] = alpha * own[0, i]
            return carry

        lax.fori_loop(0, slabs, slab, 0)
        acc[...] = jnp.zeros_like(acc)

    scaled = [w * scale[0] for w in weights]
    border = Borders(scaled)
    rt[...] = part[...]
    for c in range(3):
        add_borders(border, rt, low, high, c, 0, levels)

    sh = Shifts((levels, LANES))
    is_first = jnp.where(x == 0, 1.0, 0.0).astype(jnp.float32)
    is_last = jnp.where(x == slabs - 1, 1.0, 0.0).astype(jnp.float32)

    def at(c, dx, j):
        return scratch[c, x + 1 + dx, j % NJ, pl.ds(OWN, levels), :]

    s1 = s2 = s3 = None
    for c in range(3):
        cache = {}

        def products(j):
            j = j % NJ
            if j not in cache:
                value = at(c, 0, j)
                y = (alpha * own[1, x, :, cols(j)]) * value
                z = (alpha * own[2, x, :, cols(j)]) * value
                s = beta * value
                cache[j] = (y + s, y - s, z + s, z - s)
            return cache[j]

        for j in range(NJ):
            here = at(c, 0, j)
            (_, ym0, zp0, zm0) = products(j - 1)
            (yp1, ym1, zp1, zm1) = products(j)
            (yp2, _, zp2, zm2) = products(j + 1)
            total = (6.0 * beta) * here - rate(scratch, c, x + 1, j, levels, scaled)
            nxt, prv = at(c, 1, j), at(c, -1, j)
            total = total - (flow[x + 2, :, cols(j)] + beta) * nxt
            total = total + (flow[x, :, cols(j)] - beta) * prv
            total = total - sh.y_next(yp1, yp2) + sh.y_prev(ym0, ym1)
            total = total - sh.z_next(j, zp0, zp1, zp2) + sh.z_prev(j, zm0, zm1, zm2)
            dots = None
            for k in range(3):
                diff = grad[c * 3 + k, 0, :, cols(j)]
                if c == 0:
                    diff = diff + (is_last * right[k, :, cols(j)] - is_first * left[k, :, cols(j)])
                term = at(k, 0, j) * diff
                dots = term if dots is None else dots + term
            total = total + alpha * dots
            q = rt[c, 0, :, cols(j)]
            t1, t2, t3 = here * q, q * q, total * q
            s1 = t1 if s1 is None else s1 + t1
            s2 = t2 if s2 is None else s2 + t2
            s3 = t3 if s3 is None else s3 + t3
            base[c, 0, :, cols(j)] = own[c, x, :, cols(j)] - step_size * total
    acc[0] += s1
    acc[1] += s2
    acc[2] += s3

    @pl.when(x == slabs - 1)
    def _():
        sums[...] = acc[...]
        pltpu.make_async_copy(res, res_out, sem).wait()


def closing_kernel(scale, part, rt, low, high, left, right, partial, base, sums):
    slabs, levels = part.shape[1], part.shape[2]
    border = Borders([w * scale[0] for w in weights])

    def slab(x, total):
        for c in range(3):
            base[c, x] = part[c, x]
            for j in range(0, NJ, 2):
                below, above = border.from_low(low, c, x, j), border.from_high(high, c, x, j)
                for k in range(2):
                    for row, take in ((0, below[k]), (levels - 4, above[k])):
                        rows = pl.ds(row, 4)
                        total = total - take * rt[c, x, rows, cols(j + k)]
                        base[c, x, rows, cols(j + k)] += step_size * take
        return total

    inner = lax.fori_loop(0, slabs, slab, jnp.zeros((4, LANES), jnp.float32))

    def edge(sign, message, x):
        total = jnp.zeros((levels, LANES), jnp.float32)
        for c in range(3):
            for j in range(NJ):
                extra = message[c, :, cols(j)]
                total = total + extra * rt[c, x, :, cols(j)]
                base[c, x, :, cols(j)] = base[c, x, :, cols(j)] - (sign * step_size) * extra
        return sign * total

    outer = edge(1.0, left, 0) + edge(-1.0, right, slabs - 1)
    lane = lax.broadcasted_iota(jnp.int32, (1, LANES), 1)
    row = jnp.zeros((1, LANES), jnp.float32)
    for k in range(3):
        value = jnp.sum(partial[k]) if k < 2 else jnp.sum(partial[k] + outer) + jnp.sum(inner)
        row = jnp.where(lane == k, value, row)
    sums[...] = jnp.broadcast_to(row[None], sums.shape)


def update_kernel(cells, period, gathered, base, rt, out, pgrad, buffer, sem):
    slabs, levels = base.shape[1], base.shape[2]
    row = jnp.sum(gathered[...], axis=0)
    s1, s2, s3 = row[0, 0], row[0, 1], row[0, 2]
    ratio = jnp.full((1, LANES), step_size * s3, jnp.float32) / jnp.full((1, LANES), s2, jnp.float32)
    factor = jnp.broadcast_to(ratio, (levels, LANES))
    pgrad[...] = jnp.full((1, LANES), -s1, jnp.float32) / jnp.full((1, LANES), period[0] * cells, jnp.float32)

    def slab(x, carry):
        for c in range(3):
            for j in range(NJ):
                buffer[c, x, :, cols(j)] = base[c, x, :, cols(j)] + factor * rt[c, x, :, cols(j)]
        pltpu.make_async_copy(buffer.at[:, x], out.at[:, x], sem).start()
        return carry

    lax.fori_loop(0, slabs, slab, 0)
    pltpu.make_async_copy(buffer, out, sem).wait()


def ring(axis):
    count = lax.axis_size(axis)
    up = [(i, (i + 1) % count) for i in range(count)]
    return up, [(j, i) for i, j in up]


def exchange(first, last, down, up):
    tm_up, tm_down = ring(TM)
    space_up, space_down = ring(SPACE)
    left = lax.ppermute(up, SPACE, space_up)
    right = lax.ppermute(down, SPACE, space_down)
    low = lax.ppermute(last, TM, tm_up)
    high = lax.ppermute(first, TM, tm_down)
    return low, high, left, right


def step(velocity, period, wavenumber):
    levels, _, slabs, _ = velocity.shape
    devices = lax.axis_size(ALL)
    total_levels = levels * lax.axis_size(TM)
    grid_first = slabs * lax.axis_size(SPACE)
    spacing = 2.0 * math.pi / NY
    u = jnp.transpose(velocity, (1, 2, 0, 3))
    scale = total_levels / period
    row_index = jnp.arange(NY, dtype=jnp.float32)
    profile = jnp.sin(wavenumber[0].astype(jnp.float32) * (2.0 * math.pi / NY) * row_index)
    forcing = jnp.repeat(profile, NZ).reshape(1, NC)

    vmem = pl.BlockSpec(memory_space=pltpu.VMEM)
    smem = pl.BlockSpec(memory_space=pltpu.SMEM)
    hbm = pl.BlockSpec(memory_space=pl.ANY)
    slab3 = pl.BlockSpec((3, 1, levels, NC), lambda i: (0, i, 0, 0))
    slab9 = pl.BlockSpec((9, 1, levels, NC), lambda i: (0, i, 0, 0))
    four3 = pl.BlockSpec((3, 1, 4, NC), lambda i: (0, i, 0, 0))
    sums3 = pl.BlockSpec((3, levels, LANES), lambda i: (0, 0, 0))

    def shape(*dims):
        return jax.ShapeDtypeStruct(dims, jnp.float32)

    def params(mib):
        return pltpu.CompilerParams(vmem_limit_bytes=mib << 20)

    field = shape(3, slabs, levels, NC)
    four = shape(3, slabs, 4, NC)
    edge = shape(3, levels, NC)
    padded = pltpu.VMEM((3, slabs + 2, NJ, ROWS, LANES), jnp.float32)
    work = pl.CostEstimate(flops=30_000_000, bytes_accessed=40_000_000, transcendentals=0)
    little = pl.CostEstimate(flops=3_000_000, bytes_accessed=6_000_000, transcendentals=0)

    down, up = pl.pallas_call(
        edges_kernel,
        in_specs=[pl.BlockSpec(memory_space=pltpu.HBM)],
        out_specs=[vmem] * 2,
        out_shape=[edge, edge],
        scratch_shapes=[pltpu.SemaphoreType.DMA((2,))],
        compiler_params=params(60),
        cost_estimate=little,
        name="edges",
    )(u)
    first, last = pl.pallas_call(
        ends_kernel,
        in_specs=[vmem],
        out_specs=[vmem] * 2,
        out_shape=[four, four],
        compiler_params=params(8),
        cost_estimate=little,
        name="ends",
    )(u)
    low, high, left, right = exchange(first, last, down, up)
    res_part, rt_part, grad = pl.pallas_call(
        lambda *refs: residual_kernel(spacing, *refs),
        grid=(slabs,),
        in_specs=[smem, vmem, vmem],
        out_specs=[slab3, slab3, slab9],
        out_shape=[field, field, shape(9, slabs, levels, NC)],
        scratch_shapes=[padded],
        compiler_params=params(16),
        cost_estimate=work,
        name="residual",
    )(scale, u, forcing)

    res, first, last, down, up = pl.pallas_call(
        lambda *refs: joined_kernel(spacing, *refs),
        in_specs=[smem] + [vmem] * 6,
        out_specs=[vmem] * 5,
        out_shape=[field, four, four, edge, edge],
        compiler_params=params(18),
        cost_estimate=little,
        name="joined",
    )(scale, res_part, u, low, high, left, right)
    res_low, res_high, res_left, res_right = exchange(first, last, down, up)
    base_part, rt, partial, res_out = pl.pallas_call(
        lambda *refs: descent_kernel(spacing, *refs),
        grid=(slabs,),
        in_specs=[smem, vmem, vmem, vmem, vmem, slab3, slab9, four3, four3],
        out_specs=[slab3, slab3, sums3, hbm],
        out_shape=[field, field, shape(3, levels, LANES), field],
        scratch_shapes=[
            padded,
            pltpu.VMEM((slabs + 2, levels, NC), jnp.float32),
            pltpu.VMEM((3, levels, LANES), jnp.float32),
            pltpu.SemaphoreType.DMA,
        ],
        compiler_params=params(22),
        cost_estimate=work,
        name="descent",
    )(scale, u, res, left, right, rt_part, grad, low, high)
    base, sums = pl.pallas_call(
        closing_kernel,
        in_specs=[smem] + [vmem] * 7,
        out_specs=[vmem, vmem],
        out_shape=[field, shape(devices, 1, LANES)],
        compiler_params=params(16),
        cost_estimate=little,
        name="closing",
    )(scale, base_part, rt, res_low, res_high, res_left, res_right, partial)

    gathered = lax.all_to_all(sums, ALL, 0, 0)
    cells = 3.0 * total_levels * grid_first * NY * NZ
    updated, pgrad = pl.pallas_call(
        lambda *refs: update_kernel(cells, *refs),
        in_specs=[smem, vmem, vmem, vmem],
        out_specs=[hbm, vmem],
        out_shape=[field, shape(1, LANES)],
        scratch_shapes=[pltpu.VMEM((3, slabs, levels, NC), jnp.float32), pltpu.SemaphoreType.DMA],
        compiler_params=params(14),
        cost_estimate=little,
        name="update",
    )(period, gathered, base, rt)
    back = (2, 0, 1, 3)
    return jnp.transpose(updated, back), jnp.transpose(res_out, back), pgrad[0, :1]


def solution(mesh):
    split = Mesh(mesh.devices.reshape(2, 4, 2, 2, 4), ALL)
    in_specs = (P(TM, None, SPACE, None), P(), P())
    out_specs = (P(TM, None, SPACE, None), P(TM, None, SPACE, None), P())
    return jax.shard_map(step, mesh=split, in_specs=in_specs, out_specs=out_specs, check_vma=False)
```

```python
import math

import jax
import jax.numpy as jnp
from jax import lax
from jax.experimental import pallas as pl
from jax.experimental.pallas import tpu as pltpu
from jax.sharding import Mesh
from jax.sharding import PartitionSpec as P


NY = 48
NZ = 48
NC = NY * NZ
LANES = 128
NJ = NC // LANES
TM = ("tm_0", "tm_1", "tm_2")
SPACE = ("space_0", "space_1")
ALL = TM + SPACE

weights = (0.8, -0.2, 4.0 / 105.0, -1.0 / 280.0)
viscosity = 0.02
step_size = 0.15

ROWS = 32
OWN = 8


def cols(j):
    return pl.ds(j * LANES, LANES)


def roll(x, shift):
    return pltpu.roll(x, shift % LANES, x.ndim - 1)


class Shifts:
    def __init__(self, shape):
        self.lane = lax.broadcasted_iota(jnp.int32, shape, len(shape) - 1)

    def y_next(self, here, after):
        return roll(jnp.where(self.lane < NZ, after, here), -NZ)

    def y_prev(self, before, here):
        return roll(jnp.where(self.lane >= LANES - NZ, before, here), NZ)

    def column(self, j, value):
        base = (j * LANES) % NZ
        mask = None
        for lane in range(LANES):
            if (base + lane) % NZ == value:
                one = self.lane == lane
                mask = one if mask is None else jnp.logical_or(mask, one)
        return mask

    def z_next(self, j, before, here, after):
        base = (j * LANES) % NZ
        straight = here if (base + LANES) % NZ == 0 else jnp.where(self.lane == 0, after, here)
        first = (NZ - 1 - base) % NZ
        wrap = here if first >= NZ - 1 else jnp.where(self.lane >= LANES - (NZ - 1), before, here)
        return jnp.where(self.column(j, NZ - 1), roll(wrap, NZ - 1), roll(straight, -1))

    def z_prev(self, j, before, here, after):
        base = (j * LANES) % NZ
        straight = here if base == 0 else jnp.where(self.lane == LANES - 1, before, here)
        last = LANES - 1 - (base + LANES - 1) % NZ
        wrap = here if last + NZ - 1 < LANES else jnp.where(self.lane < NZ - 1, after, here)
        return jnp.where(self.column(j, 0), roll(wrap, -(NZ - 1)), roll(straight, 1))


def rate(ref, c, x, j, levels, scaled):
    total = None
    for m in range(1, 5):
        ahead = ref[c, x, j, pl.ds(OWN + m, levels), :]
        behind = ref[c, x, j, pl.ds(OWN - m, levels), :]
        term = scaled[m - 1] * (ahead - behind)
        total = term if total is None else total + term
    return total


def fill(scratch, own):
    slabs, levels = own.shape[1], own.shape[2]
    zero = jnp.zeros((levels, LANES), jnp.float32)
    edge = jnp.zeros((4, LANES), jnp.float32)

    def slab(x, carry):
        for c in range(3):
            for j in range(NJ):
                scratch[c, x + 1, j, pl.ds(OWN, levels), :] = own[c, x, :, cols(j)]
                scratch[c, x + 1, j, pl.ds(OWN - 4, 4), :] = edge
                scratch[c, x + 1, j, pl.ds(OWN + levels, 4), :] = edge
        return carry

    lax.fori_loop(0, slabs, slab, 0)
    for c in range(3):
        for j in range(NJ):
            scratch[c, 0, j, pl.ds(OWN, levels), :] = zero
            scratch[c, slabs + 1, j, pl.ds(OWN, levels), :] = zero


class Borders:
    def __init__(self, scaled):
        row = lax.broadcasted_iota(jnp.int32, (8, LANES), 0) % 4
        zero = jnp.zeros((8, LANES), jnp.float32)
        self.low = [jnp.where(row < m, zero - scaled[m - 1], zero) for m in range(1, 5)]
        self.high = [jnp.where(row >= 4 - m, zero + scaled[m - 1], zero) for m in range(1, 5)]

    def pair(self, coefficients, sign, message, c, x, j):
        eight = jnp.concatenate([message[c, x, :, cols(j)], message[c, x, :, cols(j + 1)]], axis=0)
        total = coefficients[3] * eight
        for m in range(1, 4):
            total = total + coefficients[m - 1] * pltpu.roll(eight, (sign * (4 - m)) % 8, 0)
        return total[:4], total[4:]

    def from_low(self, message, c, x, j):
        return self.pair(self.low, -1, message, c, x, j)

    def from_high(self, message, c, x, j):
        return self.pair(self.high, 1, message, c, x, j)


def add_borders(border, ref, low, high, c, x, levels):
    for j in range(0, NJ, 2):
        below, above = border.from_low(low, c, x, j), border.from_high(high, c, x, j)
        for k in range(2):
            ref[c, x, pl.ds(0, 4), cols(j + k)] += below[k]
            ref[c, x, pl.ds(levels - 4, 4), cols(j + k)] += above[k]


def level_parity():
    return lax.axis_index(TM[-1])


def slab_parity():
    return lax.rem(lax.axis_index(SPACE[-1]), 2)


def by_parity(parity, body, odd, even):
    @pl.when(parity == 1)
    def _():
        body(even, odd)

    @pl.when(parity == 0)
    def _():
        body(odd, even)


def edges_kernel(own, odd, even, sems):
    slabs = own.shape[1]
    upper = slab_parity() * (slabs - 1)
    copies = [
        pltpu.make_async_copy(own.at[:, upper], odd, sems.at[0]),
        pltpu.make_async_copy(own.at[:, slabs - 1 - upper], even, sems.at[1]),
    ]
    for copy in copies:
        copy.start()
    for copy in copies:
        copy.wait()


def ends_kernel(own, odd, even):
    levels = own.shape[2]

    def body(first, last):
        first[...] = own[:, :, pl.ds(0, 4), :]
        last[...] = own[:, :, pl.ds(levels - 4, 4), :]

    by_parity(level_parity(), body, odd, even)


def residual_kernel(spacing, total_levels, period, wavenumber, own, res, rt, grad, scratch, forcing, factors):
    levels = own.shape[2]
    x = pl.program_id(0)

    @pl.when(x == 0)
    def _():
        fill(scratch, own)
        inverse_step = (total_levels / jnp.broadcast_to(period[...], (1, LANES)))[0, 0]
        for m in range(4):
            factors[m] = weights[m] * inverse_step
        turn = jnp.broadcast_to(wavenumber[...], (1, LANES)).astype(jnp.float32) * (2.0 * math.pi / NY)
        lane = lax.broadcasted_iota(jnp.int32, (1, LANES), 1).astype(jnp.float32)
        for j in range(NJ):
            forcing[:, cols(j)] = jnp.sin(turn * jnp.floor((lane + (j * LANES + 0.5)) * (1.0 / NZ)))

    scaled = [factors[m] for m in range(4)]
    alpha = 1.0 / (2.0 * spacing)
    beta = viscosity / spacing**2
    sh = Shifts((levels, LANES))

    def at(c, dx, j):
        return scratch[c, x + 1 + dx, j % NJ, pl.ds(OWN, levels), :]

    for j in range(NJ):
        vel = [alpha * at(a, 0, j) for a in range(3)]
        for c in range(3):
            here, before, after = at(c, 0, j), at(c, 0, j - 1), at(c, 0, j + 1)
            pairs = (
                (at(c, 1, j), at(c, -1, j)),
                (sh.y_next(here, after), sh.y_prev(before, here)),
                (sh.z_next(j, before, here, after), sh.z_prev(j, before, here, after)),
            )
            q = rate(scratch, c, x + 1, j, levels, scaled)
            total = q + (6.0 * beta) * here
            near = None
            for a, (nxt, prv) in enumerate(pairs):
                diff = nxt - prv
                grad[a * 3 + c, 0, :, cols(j)] = diff
                total = total + vel[a] * diff
                both = nxt + prv
                near = both if near is None else near + both
            total = total - beta * near
            if c == 0:
                total = total - forcing[:, cols(j)]
            res[c, 0, :, cols(j)] = total
            rt[c, 0, :, cols(j)] = q


def joined_kernel(spacing, scale, part, own, tm_odd, tm_even, space_odd, space_even, res, out_tm_odd, out_tm_even, out_space_odd, out_space_even):
    slabs, levels = own.shape[1], own.shape[2]
    alpha = 1.0 / (2.0 * spacing)
    beta = viscosity / spacing**2
    border = Borders([w * scale[0] for w in weights])

    def inner(low, high):
        def slab(x, carry):
            for c in range(3):
                res[c, x] = part[c, x]
                add_borders(border, res, low, high, c, x, levels)
            return carry

        lax.fori_loop(0, slabs, slab, 0)

    by_parity(level_parity(), inner, tm_odd, tm_even)

    def outer(lower, upper):
        (left, down), (right, up) = lower, upper
        for c in range(3):
            for j in range(NJ):
                plus = alpha * own[0, 0, :, cols(j)] + beta
                value = res[c, 0, :, cols(j)] - plus * left[c, :, cols(j)]
                res[c, 0, :, cols(j)] = value
                down[c, :, cols(j)] = plus * value
                minus = alpha * own[0, slabs - 1, :, cols(j)] - beta
                value = res[c, slabs - 1, :, cols(j)] + minus * right[c, :, cols(j)]
                res[c, slabs - 1, :, cols(j)] = value
                up[c, :, cols(j)] = minus * value

    by_parity(slab_parity(), outer, (space_odd, out_space_odd), (space_even, out_space_even))

    def ends(first, last):
        first[...] = res[:, :, pl.ds(0, 4), :]
        last[...] = res[:, :, pl.ds(levels - 4, 4), :]

    by_parity(level_parity(), ends, out_tm_odd, out_tm_even)


def descent_kernel(spacing, scale, own, res, space_odd, space_even, part, grad, tm_odd, tm_even, base, rt, sums, res_out, scratch, flow, acc, sem):
    levels = own.shape[2]
    slabs = own.shape[1]
    x = pl.program_id(0)
    alpha = 1.0 / (2.0 * spacing)
    beta = viscosity / spacing**2

    @pl.when(x == 0)
    def _():
        pltpu.make_async_copy(res, res_out, sem).start()
        fill(scratch, res)
        flow[0] = jnp.zeros_like(flow[0])
        flow[slabs + 1] = jnp.zeros_like(flow[0])

        def slab(i, carry):
            flow[i + 1] = alpha * own[0, i]
            return carry

        lax.fori_loop(0, slabs, slab, 0)
        acc[...] = jnp.zeros_like(acc)

    scaled = [w * scale[0] for w in weights]
    border = Borders(scaled)
    rt[...] = part[...]

    def borders(low, high):
        for c in range(3):
            add_borders(border, rt, low, high, c, 0, levels)

    by_parity(level_parity(), borders, tm_odd, tm_even)
    sh = Shifts((levels, LANES))
    odd = slab_parity() == 1
    lower = jnp.where(x == 0, -1.0, 0.0).astype(jnp.float32)
    upper = jnp.where(x == slabs - 1, 1.0, 0.0).astype(jnp.float32)
    from_odd, from_even = jnp.where(odd, upper, lower), jnp.where(odd, lower, upper)

    def at(c, dx, j):
        return scratch[c, x + 1 + dx, j % NJ, pl.ds(OWN, levels), :]

    s1 = s2 = s3 = None
    for c in range(3):
        cache = {}

        def products(j):
            j = j % NJ
            if j not in cache:
                value = at(c, 0, j)
                y = (alpha * own[1, x, :, cols(j)]) * value
                z = (alpha * own[2, x, :, cols(j)]) * value
                s = beta * value
                cache[j] = (y + s, y - s, z + s, z - s)
            return cache[j]

        for j in range(NJ):
            here = at(c, 0, j)
            (_, ym0, zp0, zm0) = products(j - 1)
            (yp1, ym1, zp1, zm1) = products(j)
            (yp2, _, zp2, zm2) = products(j + 1)
            total = (6.0 * beta) * here - rate(scratch, c, x + 1, j, levels, scaled)
            nxt, prv = at(c, 1, j), at(c, -1, j)
            total = total - (flow[x + 2, :, cols(j)] + beta) * nxt
            total = total + (flow[x, :, cols(j)] - beta) * prv
            total = total - sh.y_next(yp1, yp2) + sh.y_prev(ym0, ym1)
            total = total - sh.z_next(j, zp0, zp1, zp2) + sh.z_prev(j, zm0, zm1, zm2)
            dots = None
            for k in range(3):
                diff = grad[c * 3 + k, 0, :, cols(j)]
                if c == 0:
                    diff = diff + (from_odd * space_odd[k, :, cols(j)] + from_even * space_even[k, :, cols(j)])
                term = at(k, 0, j) * diff
                dots = term if dots is None else dots + term
            total = total + alpha * dots
            q = rt[c, 0, :, cols(j)]
            t1, t2, t3 = here * q, q * q, total * q
            s1 = t1 if s1 is None else s1 + t1
            s2 = t2 if s2 is None else s2 + t2
            s3 = t3 if s3 is None else s3 + t3
            base[c, 0, :, cols(j)] = own[c, x, :, cols(j)] - step_size * total
    acc[0] += s1
    acc[1] += s2
    acc[2] += s3

    @pl.when(x == slabs - 1)
    def _():
        sums[...] = acc[...]
        pltpu.make_async_copy(res, res_out, sem).wait()


def closing_kernel(scale, part, rt, tm_odd, tm_even, space_odd, space_even, partial, base, sums, inner, outer):
    slabs, levels = part.shape[1], part.shape[2]
    border = Borders([w * scale[0] for w in weights])

    def middle(low, high):
        def slab(x, total):
            for c in range(3):
                base[c, x] = part[c, x]
                for j in range(0, NJ, 2):
                    below, above = border.from_low(low, c, x, j), border.from_high(high, c, x, j)
                    for k in range(2):
                        for row, take in ((0, below[k]), (levels - 4, above[k])):
                            rows = pl.ds(row, 4)
                            total = total - take * rt[c, x, rows, cols(j + k)]
                            base[c, x, rows, cols(j + k)] += step_size * take
            return total

        inner[...] = lax.fori_loop(0, slabs, slab, jnp.zeros((4, LANES), jnp.float32))

    by_parity(level_parity(), middle, tm_odd, tm_even)

    def edges(left, right):
        total = jnp.zeros((levels, LANES), jnp.float32)
        for sign, message, x in ((1.0, left, 0), (-1.0, right, slabs - 1)):
            for c in range(3):
                for j in range(NJ):
                    extra = sign * message[c, :, cols(j)]
                    total = total + extra * rt[c, x, :, cols(j)]
                    base[c, x, :, cols(j)] = base[c, x, :, cols(j)] - step_size * extra
        outer[...] = total

    by_parity(slab_parity(), edges, space_odd, space_even)
    lane = lax.broadcasted_iota(jnp.int32, (1, LANES), 1)
    row = jnp.zeros((1, LANES), jnp.float32)
    for k in range(3):
        value = jnp.sum(partial[k]) if k < 2 else jnp.sum(partial[k] + outer[...]) + jnp.sum(inner[...])
        row = jnp.where(lane == k, value, row)
    sums[...] = jnp.broadcast_to(row[None], sums.shape)


def update_kernel(cells, period, gathered, base, rt, out, pgrad, buffer, sem):
    slabs, levels = base.shape[1], base.shape[2]
    row = jnp.sum(gathered[...], axis=0)
    s1, s2, s3 = row[0, 0], row[0, 1], row[0, 2]
    ratio = jnp.full((1, LANES), step_size * s3, jnp.float32) / jnp.full((1, LANES), s2, jnp.float32)
    factor = jnp.broadcast_to(ratio, (levels, LANES))
    pgrad[...] = jnp.full((1, LANES), -s1, jnp.float32) / jnp.full((1, LANES), period[0] * cells, jnp.float32)

    def slab(x, carry):
        for c in range(3):
            for j in range(NJ):
                buffer[c, x, :, cols(j)] = base[c, x, :, cols(j)] + factor * rt[c, x, :, cols(j)]
        pltpu.make_async_copy(buffer.at[:, x], out.at[:, x], sem).start()
        return carry

    lax.fori_loop(0, slabs, slab, 0)
    pltpu.make_async_copy(buffer, out, sem).wait()


def pairing(axis, odd):
    count = lax.axis_size(axis)
    pairs = []
    for i in range(odd, count, 2):
        other = (i + 1) % count
        pairs += [(i, other), (other, i)]
    return pairs


def send(array, axis, odd):
    return lax.ppermute(array, axis, pairing(axis, odd))


def exchange(tm_odd, tm_even, space_odd, space_even):
    return (send(tm_odd, TM, 1), send(tm_even, TM, 0), send(space_odd, SPACE, 1), send(space_even, SPACE, 0))


def step(velocity, period, wavenumber):
    levels, _, slabs, _ = velocity.shape
    devices = lax.axis_size(ALL)
    total_levels = levels * lax.axis_size(TM)
    grid_first = slabs * lax.axis_size(SPACE)
    spacing = 2.0 * math.pi / NY
    u = jnp.transpose(velocity, (1, 2, 0, 3))
    scale = total_levels / period
    vmem = pl.BlockSpec(memory_space=pltpu.VMEM)
    smem = pl.BlockSpec(memory_space=pltpu.SMEM)
    hbm = pl.BlockSpec(memory_space=pl.ANY)
    slab3 = pl.BlockSpec((3, 1, levels, NC), lambda i: (0, i, 0, 0))
    slab9 = pl.BlockSpec((9, 1, levels, NC), lambda i: (0, i, 0, 0))
    four3 = pl.BlockSpec((3, 1, 4, NC), lambda i: (0, i, 0, 0))
    sums3 = pl.BlockSpec((3, levels, LANES), lambda i: (0, 0, 0))

    def shape(*dims):
        return jax.ShapeDtypeStruct(dims, jnp.float32)

    def params(mib):
        return pltpu.CompilerParams(vmem_limit_bytes=mib << 20)

    field = shape(3, slabs, levels, NC)
    four = shape(3, slabs, 4, NC)
    edge = shape(3, levels, NC)
    padded = pltpu.VMEM((3, slabs + 2, NJ, ROWS, LANES), jnp.float32)
    work = pl.CostEstimate(flops=30_000_000, bytes_accessed=40_000_000, transcendentals=0)
    little = pl.CostEstimate(flops=3_000_000, bytes_accessed=6_000_000, transcendentals=0)

    space_odd, space_even = pl.pallas_call(
        edges_kernel,
        in_specs=[pl.BlockSpec(memory_space=pltpu.HBM)],
        out_specs=[vmem] * 2,
        out_shape=[edge, edge],
        scratch_shapes=[pltpu.SemaphoreType.DMA((2,))],
        compiler_params=params(60),
        cost_estimate=little,
        name="edges",
    )(u)
    tm_odd, tm_even = pl.pallas_call(
        ends_kernel,
        in_specs=[vmem],
        out_specs=[vmem] * 2,
        out_shape=[four, four],
        compiler_params=params(8),
        cost_estimate=little,
        name="ends",
    )(u)
    halo = exchange(tm_odd, tm_even, space_odd, space_even)
    res_part, rt_part, grad = pl.pallas_call(
        lambda *refs: residual_kernel(spacing, total_levels, *refs),
        grid=(slabs,),
        in_specs=[vmem, vmem, vmem],
        out_specs=[slab3, slab3, slab9],
        out_shape=[field, field, shape(9, slabs, levels, NC)],
        scratch_shapes=[padded, pltpu.VMEM((1, NC), jnp.float32), pltpu.SMEM((4,), jnp.float32)],
        compiler_params=params(16),
        cost_estimate=work,
        name="residual",
    )(period.reshape(1, 1), wavenumber.reshape(1, 1), u)

    res, *messages = pl.pallas_call(
        lambda *refs: joined_kernel(spacing, *refs),
        in_specs=[smem] + [vmem] * 6,
        out_specs=[vmem] * 5,
        out_shape=[field, four, four, edge, edge],
        compiler_params=params(18),
        cost_estimate=little,
        name="joined",
    )(scale, res_part, u, *halo)
    res_halo = exchange(*messages)
    base_part, rt, partial, res_out = pl.pallas_call(
        lambda *refs: descent_kernel(spacing, *refs),
        grid=(slabs,),
        in_specs=[smem, vmem, vmem, vmem, vmem, slab3, slab9, four3, four3],
        out_specs=[slab3, slab3, sums3, hbm],
        out_shape=[field, field, shape(3, levels, LANES), field],
        scratch_shapes=[
            padded,
            pltpu.VMEM((slabs + 2, levels, NC), jnp.float32),
            pltpu.VMEM((3, levels, LANES), jnp.float32),
            pltpu.SemaphoreType.DMA,
        ],
        compiler_params=params(22),
        cost_estimate=work,
        name="descent",
    )(scale, u, res, *halo[2:], rt_part, grad, *halo[:2])
    base, sums = pl.pallas_call(
        closing_kernel,
        in_specs=[smem] + [vmem] * 7,
        out_specs=[vmem, vmem],
        out_shape=[field, shape(devices, 1, LANES)],
        scratch_shapes=[pltpu.VMEM((4, LANES), jnp.float32), pltpu.VMEM((levels, LANES), jnp.float32)],
        compiler_params=params(16),
        cost_estimate=little,
        name="closing",
    )(scale, base_part, rt, *res_halo, partial)

    gathered = lax.all_to_all(sums, ALL, 0, 0)
    cells = 3.0 * total_levels * grid_first * NY * NZ
    updated, pgrad = pl.pallas_call(
        lambda *refs: update_kernel(cells, *refs),
        in_specs=[smem, vmem, vmem, vmem],
        out_specs=[hbm, vmem],
        out_shape=[field, shape(1, LANES)],
        scratch_shapes=[pltpu.VMEM((3, slabs, levels, NC), jnp.float32), pltpu.SemaphoreType.DMA],
        compiler_params=params(14),
        cost_estimate=little,
        name="update",
    )(period, gathered, base, rt)
    back = (2, 0, 1, 3)
    return jnp.transpose(updated, back), jnp.transpose(res_out, back), pgrad[0, :1]


def solution(mesh):
    split = Mesh(mesh.devices.reshape(2, 4, 2, 2, 4), ALL)
    in_specs = (P(TM, None, SPACE, None), P(), P())
    out_specs = (P(TM, None, SPACE, None), P(TM, None, SPACE, None), P())
    return jax.shard_map(step, mesh=split, in_specs=in_specs, out_specs=out_specs, check_vma=False)
```
